256 devices in a mesh: seq: 32 (over y_lo, z, core), tp: 4 (over x), dp: 2 (over y_hi).
Axes of the slice: x: 4, y: 4 (y_hi: 2, y_lo: 2; y = y_hi * 2 + y_lo), z: 8, core: 2. Of those that a mesh axis runs over, the one named last changes fastest.
Arguments:
- query_gate: bfloat16 [2, 8192, 4096], P('dp', 'seq', 'tp'), may hold values from -6 to 6
- key_gate: bfloat16 [2, 8192, 4096], P('dp', 'seq', 'tp'), may hold values from -6 to 6
- value_input: bfloat16 [2, 8192, 4096], P('dp', 'seq', 'tp'), may hold values from -6 to 6
- filter_taps: bfloat16 [4096, 128], P('tp'), may hold values from -0.5 to 0.5
- skip_gain: float32 [4096], P('tp'), may hold values from -1 to 1
- out_weight: bfloat16 [4096, 4096], P('tp', 'dp'), may hold values from -0.09375 to 0.09375
- cotangent: bfloat16 [2, 8192, 4096], P('dp', 'seq', 'tp'), may hold values from -6 to 6
Outputs:
- grad_query: bfloat16 [2, 8192, 4096], P('dp', 'seq', 'tp')
- grad_key: bfloat16 [2, 8192, 4096], P('dp', 'seq', 'tp')
- grad_value: bfloat16 [2, 8192, 4096], P('dp', 'seq', 'tp')
- grad_filter: float32 [4096, 128], P('tp')
- grad_skip: float32 [4096], P('tp')
- grad_weight: float32 [4096, 4096], P(('seq', 'dp'), 'tp')
The draws below stay inside these ranges and needn't reach their ends.
All inputs are finite; a program needn't handle non-finite values.
Results may differ from the reference program's by a relative error of at most 0.0095.
Values may be sent and summed in bfloat16 or wider, within the bound.
A program may use at most 192 MiB of HBM per device.

```python
import math
import jax
import jax.numpy as jnp
from jax import lax

D = 4096
TAPS = 128
LENGTH = 8192
SEQS = 2


def draw_cotangent(key, part):
    position = jnp.arange(LENGTH, dtype=jnp.float32) / LENGTH
    values = jax.random.normal(key, (SEQS, LENGTH, D), jnp.float32) * (0.5 + position)[None, :, None]
    return jnp.clip(values, -6.0, 6.0).astype(jnp.bfloat16)


def block_levels(stream_key, extent, cuts, smallest, largest):
    factor_of, own = 1.0, jax.random.fold_in(stream_key, 6)
    for dim, shards_of in cuts:
        heights = jnp.exp(jax.random.uniform(jax.random.fold_in(own, dim), (shards_of,), jnp.float32, smallest / len(cuts), largest / len(cuts)))
        factor_of = factor_of * jnp.repeat(heights, extent[dim] // shards_of).reshape([-1 if axis == dim else 1 for axis in range(len(extent))])
    return factor_of


def centred(own_key, dims, deviation, limit, cuts=(), held_as=jnp.bfloat16):
    factor_of = block_levels(own_key, dims, cuts, -0.22, 0.18) if cuts else 1.0
    drawn = jax.random.normal(own_key, dims, jnp.float32) * deviation * factor_of
    return jnp.minimum(jnp.maximum(drawn, -limit), limit).astype(held_as)


def setup_inputs(seed: int = 0) -> dict:
    keys = jax.random.split(jax.random.key(seed), 8)
    query_gate = centred(keys[0], (SEQS, LENGTH, D), 1.0, 6.0, ((0, 2), (1, 32), (2, 4)))
    key_gate = centred(keys[1], (SEQS, LENGTH, D), 1.0, 6.0, ((0, 2), (1, 32), (2, 4)))
    value_input = centred(keys[2], (SEQS, LENGTH, D), 1.0, 6.0, ((0, 2), (1, 32), (2, 4)))
    filter_taps = centred(keys[3], (D, TAPS), TAPS ** -0.5, 0.5, ((0, 4),))
    skip_gain = jnp.clip(jax.random.uniform(keys[4], (D,), jnp.float32, -1.0, 1.0) * block_levels(keys[4], (D,), ((0, 4),), -0.4, 0.0), -1.0, 1.0)
    out_weight = centred(keys[5], (D, D), D ** -0.5, 0.09375, ((0, 4), (1, 2)))
    cotangent = draw_cotangent(jax.random.fold_in(keys[7], 71), 0)
    return {"query_gate": query_gate, "key_gate": key_gate, "value_input": value_input, "filter_taps": filter_taps, "skip_gain": skip_gain, "out_weight": out_weight, "cotangent": cotangent}


block_rows = 32
highest = lax.Precision.HIGHEST

def taps_matrix(vector, row_count, col_count):
    channels, width_all = vector.shape
    tiled = jnp.tile(vector, (1, row_count + 1))
    skewed = tiled[:, :row_count * (width_all - 1)].reshape(channels, row_count, width_all - 1)
    return skewed[:, :, row_count - 1:row_count - 1 + col_count]

def forward_table(filter_taps):
    channels, tap_count = filter_taps.shape
    padding = jnp.zeros((channels, block_rows), filter_taps.dtype)
    vector = jnp.concatenate([padding, filter_taps[:, ::-1], padding], axis=1)
    return taps_matrix(vector, block_rows, tap_count + block_rows)

def backward_table(filter_taps):
    channels, tap_count = filter_taps.shape
    before = jnp.zeros((channels, block_rows - 1), filter_taps.dtype)
    after = jnp.zeros((channels, block_rows + 1), filter_taps.dtype)
    vector = jnp.concatenate([before, filter_taps, after], axis=1)
    return taps_matrix(vector, block_rows, tap_count + block_rows)

def windows(extended, length, tap_count):
    pieces = []
    for shift_index in range(tap_count // block_rows + 1):
        lower = shift_index * block_rows
        pieces.append(extended[lower:lower + length].reshape(length // block_rows, block_rows, extended.shape[1]))
    return jnp.concatenate(pieces, axis=1)

def lag_sums(blocks, tap_count):
    channels, row_count, col_count = blocks.shape
    flattened = blocks.reshape(channels, row_count * col_count)
    padded = jnp.concatenate([flattened, jnp.zeros((channels, row_count), blocks.dtype)], axis=1)
    diagonal = padded.reshape(channels, row_count, col_count + 1)[:, :, 1:tap_count + 1]
    return lax.optimization_barrier(jnp.sum(diagonal, axis=1))[:, ::-1]

def reference(query_gate, key_gate, value_input, filter_taps, skip_gain, out_weight, cotangent):
    norm_factor = 1.0 / math.sqrt(SEQS * LENGTH)
    band_width = min(D, 512)
    fwd_table = forward_table(filter_taps).astype(jnp.float32)
    bwd_table = backward_table(filter_taps).astype(jnp.float32)
    filter_total = jnp.zeros((D, TAPS), jnp.float32)
    skip_total = jnp.zeros((D,), jnp.float32)
    weight_total = jnp.zeros((D, D), jnp.float32)
    query_list, key_list, value_list = ([], [], [])
    for sequence in range(SEQS):
        queries = query_gate[sequence].astype(jnp.float32)
        key_rows = key_gate[sequence].astype(jnp.float32)
        value_rows = value_input[sequence].astype(jnp.float32)
        mixed = (key_rows * value_rows).astype(jnp.bfloat16)
        extended = jnp.concatenate([jnp.zeros((TAPS, D), jnp.bfloat16), mixed], axis=0).astype(jnp.float32)
        conv_parts = []
        for lower in range(0, D, band_width):
            wins = windows(extended[:, lower:lower + band_width], LENGTH, TAPS)
            conv = jnp.einsum('cab,ibc->iac', fwd_table[lower:lower + band_width], wins, precision=highest)
            conv_parts.append(conv.reshape(LENGTH, band_width))
        state = jnp.concatenate(conv_parts, axis=1) + skip_gain[None, :] * mixed.astype(jnp.float32)
        gated = (queries * state).astype(jnp.bfloat16)
        grad_gated = jnp.dot(cotangent[sequence], out_weight.T, preferred_element_type=jnp.float32)
        query_list.append((grad_gated * state).astype(jnp.bfloat16))
        signal = (grad_gated * queries).astype(jnp.bfloat16)
        signal_ext = jnp.concatenate([signal, jnp.zeros((TAPS, D), jnp.bfloat16)], axis=0).astype(jnp.float32)
        signal_blocks = signal.astype(jnp.float32).reshape(LENGTH // block_rows, block_rows, D)
        back_parts, lag_parts = ([], [])
        for lower in range(0, D, band_width):
            wins = windows(signal_ext[:, lower:lower + band_width], LENGTH, TAPS)
            back = jnp.einsum('cab,ibc->iac', bwd_table[lower:lower + band_width], wins, precision=highest)
            back_parts.append(back.reshape(LENGTH, band_width))
            fwins = windows(extended[:, lower:lower + band_width], LENGTH, TAPS)
            blocks = jnp.einsum('iac,ibc->cab', signal_blocks[:, :, lower:lower + band_width], fwins, precision=highest)
            lag_parts.append(lag_sums(blocks, TAPS))
        back = jnp.concatenate(back_parts, axis=1) + skip_gain[None, :] * signal.astype(jnp.float32)
        key_list.append((back * value_rows).astype(jnp.bfloat16))
        value_list.append((back * key_rows).astype(jnp.bfloat16))
        filter_total = filter_total + jnp.concatenate(lag_parts, axis=0)
        skip_total = skip_total + lax.optimization_barrier(jnp.sum(signal.astype(jnp.float32) * mixed.astype(jnp.float32), axis=0))
        weight_total = weight_total + jnp.dot(cotangent[sequence].T, gated, preferred_element_type=jnp.float32)
    return (jnp.stack(query_list), jnp.stack(key_list), jnp.stack(value_list), filter_total * norm_factor, skip_total * norm_factor, weight_total * norm_factor)
```

```python
import itertools
import math

import jax
import jax.numpy as jnp
import ml_dtypes
import numpy as np
from jax import lax
from jax.experimental import pallas as pl
from jax.experimental.pallas import tpu as pltpu
from jax.sharding import PartitionSpec as P

ROWS = 256
TAPS = 128
SIZE = ROWS + TAPS
HALF = SIZE // 2
CHANNELS = 1024
TILE = 256
COPIES = 200
BF16 = jnp.bfloat16
F32 = jnp.float32


def split_table(table):
    high = table.astype(ml_dtypes.bfloat16)
    low = (table - high.astype(np.float64)).astype(ml_dtypes.bfloat16)
    return np.stack([high, low])


def spectrum_tables():
    odd = 2 * np.arange(HALF) + 1

    def angles(positions):
        return np.pi * ((odd[:, None] * positions[None, :]) % (2 * SIZE)) / SIZE

    ahead = angles(np.arange(SIZE))
    forward = np.concatenate([np.cos(ahead), -np.sin(ahead)], axis=0)
    places = np.concatenate(
        [np.arange(TAPS, SIZE), np.arange(ROWS), np.arange(-TAPS, 0)]
    )
    behind = angles(places).T
    inverse = (2.0 / SIZE) * np.concatenate([np.cos(behind), -np.sin(behind)], axis=1)
    return split_table(forward), split_table(inverse)


def matmul(left, right):
    return jnp.dot(left, right, preferred_element_type=F32)


def matmul_nt(left, right):
    return lax.dot_general(
        left, right, (((1,), (1,)), ((), ())), preferred_element_type=F32
    )


def y_near(y):
    return (1 - y[0], y[1])


def y_far(y):
    return (1 - y[0], 1 - y[1])


def z_up(z):
    return z + 1 - 2 * lax.rem(z, 2)


def z_down(z):
    return lax.rem(z + 2 * lax.rem(z, 2) + 7, 8)


def z_three(z):
    return lax.rem(z + 11 - 6 * lax.rem(z, 2), 8)


def z_back_three(z):
    return lax.rem(z + 5 + 6 * lax.rem(z, 2), 8)


PLANS = (
    (("y", y_near), ("y", y_far), ("z", z_up), ("z", z_down), ("z", z_three)),
    (("y", y_far), ("y", y_near), ("z", z_down), ("z", z_up), ("z", z_back_three)),
    (("z", z_up), ("z", z_down), ("y", y_near), ("y", y_far), ("z", z_three)),
    (("z", z_down), ("z", z_up), ("y", y_far), ("y", y_near), ("z", z_back_three)),
)


def kept(rest, place):
    if not rest:
        return [place]
    return kept(rest[1:], place) + kept(rest[1:], rest[0](place))


def remaining(plan, step, axis):
    return [move for name, move in plan[step + 1 :] if name == axis]


def slots(plan, step, y, z):
    y_rest, z_rest = remaining(plan, step, "y"), remaining(plan, step, "z")
    y_list = [None] if len(y_rest) == 2 else kept(y_rest, y)
    z_list = [None] if len(z_rest) == 3 else kept(z_rest, z)
    return [(one, other) for one in y_list for other in z_list]


def slot_view(ref, quarter, slot):
    y, z = slot
    if y is None:
        return ref.at[quarter, :, z]
    if z is None:
        return ref.at[quarter, y[0], :, y[1]]
    return ref.at[quarter, y[0], z, y[1]]


def landing_shapes():
    shapes = []
    for plan in PLANS:
        for step in range(5):
            y_rest, z_rest = remaining(plan, step, "y"), remaining(plan, step, "z")
            if len(y_rest) == 2:
                shape = (2 ** len(z_rest), 2, 2, 64, TILE)
            elif len(z_rest) == 3:
                shape = (2 ** len(y_rest), 8, 64, TILE)
            else:
                shape = (2 ** (len(y_rest) + len(z_rest)), 64, TILE)
            shapes.append(shape)
    return shapes


def kernel(
    query, key, value, taps, skip, weight, cot, ahead, behind,
    out_query, out_key, out_value, out_filter, out_weight,
    full_cot, full_weight, turned, turned_away, gated, mixed, mixed_halo, signal, signal_halo,
    tap_spec, mixed_spec, state, grad_gated, partial, lag_sum, lag_out,
    near_land, lag_mid, far_land, send_sem, recv_sem, local_sem, *landing,
):
    seq, tp, dp = lax.axis_index("seq"), lax.axis_index("tp"), lax.axis_index("dp")
    core = lax.rem(seq, 2)
    z = lax.rem(lax.div(seq, 2), 8)
    y = (lax.div(seq, 16), dp)
    scale = 1.0 / math.sqrt(2 * 32 * ROWS)

    def place(y, z, core):
        return ((y[0] * 8 + z) * 2 + core, tp, y[1])

    right, left, across = lax.rem(tp + 1, 4), lax.rem(tp + 3, 4), lax.rem(tp + 2, 4)
    to_right, to_left = (seq, right, dp), (seq, left, dp)
    to_next, to_prior = (lax.rem(seq + 1, 32), tp, dp), (lax.rem(seq + 31, 32), tp, dp)
    to_core = place(y, z, 1 - core)
    member = (y[1] * 2 + y[0]) * 2 + core

    def to_member(index):
        high = lax.div(index, 4)
        return place((lax.rem(lax.div(index, 2), 2), high), z, lax.rem(index, 2))

    members = [lax.rem(member + i, 8) for i in range(8)]
    heights = [lax.rem(z + i, 8) for i in range(8)]

    barrier = pltpu.get_barrier_semaphore()
    greeted = [to_right, to_left, to_next, to_prior]
    greeted += [to_member(members[i]) for i in range(1, 8)]
    greeted += [place(y, heights[i], core) for i in range(1, 8)]
    for target in greeted:
        pl.semaphore_signal(
            barrier, inc=1, device_id=target, device_id_type=pl.DeviceIdType.MESH
        )
    pl.semaphore_wait(barrier, len(greeted))

    numbers = itertools.count()
    started = []

    def send(source, target_ref, target):
        number = next(numbers)
        copy = pltpu.make_async_remote_copy(
            src_ref=source,
            dst_ref=target_ref,
            send_sem=send_sem.at[number],
            recv_sem=recv_sem.at[number],
            device_id=target,
            device_id_type=pl.DeviceIdType.MESH,
        )
        copy.start()
        started.append(copy)
        return copy

    top, bottom = pl.ds(0, 128), pl.ds(128, 128)

    def pass_cot(owner, part, target):
        spot = full_cot.at[owner, part]
        return send(spot, spot, target)

    right_top = send(cot.at[top], full_cot.at[tp, top], to_right)
    left_bottom = send(cot.at[bottom], full_cot.at[tp, bottom], to_left)
    right_bottom = send(cot.at[bottom], full_cot.at[tp, bottom], to_right)
    left_top = send(cot.at[top], full_cot.at[tp, top], to_left)

    pieces = [(i, r) for r in range(2) for i in range(2)]
    given_row = ((1 - y[0]) * 2 + core) * 256
    taken_row = (y[0] * 2 + core) * 256
    near_row = ((1 - y[0]) * 2 + core) * 256

    def weight_spot(owner, row, piece):
        i, r = piece
        return full_weight.at[owner * 2 + i, pl.ds(pl.multiple_of(row + r * 128, 128), 128)]

    imports = []
    for i, r in pieces:
        source = weight.at[
            pl.ds(pl.multiple_of(given_row + r * 128, 128), 128), pl.ds(i * 1024, 1024)
        ]
        imports.append(send(source, weight_spot(dp, given_row, (i, r)), place(y_far(y), z, core)))

    own = [
        pltpu.make_async_copy(
            weight.at[:, pl.ds(i * 1024, 1024)], full_weight.at[dp * 2 + i], local_sem.at[i]
        )
        for i in range(2)
    ]
    for copy in own:
        copy.start()

    mixed[...] = (key[...].astype(F32) * value[...].astype(F32)).astype(BF16)
    mixed_sent = send(mixed.at[bottom], mixed_halo, to_next)
    full_cot[tp] = cot[...]

    def turn(owner):
        for i in range(4):
            mine = pl.ds(pl.multiple_of((i * 2 + core) * 128, 128), 128)
            other = pl.ds(pl.multiple_of((i * 2 + 1 - core) * 128, 128), 128)
            turned[owner * 4 + i, :, pl.ds(0, ROWS)] = full_cot[owner, :, mine].T
            turned_away[owner * 4 + i] = full_cot[owner, :, other].T
        group = pl.ds(owner * 4, 4)
        return send(turned_away.at[group], turned.at[group, :, pl.ds(ROWS, ROWS)], to_core)

    turns = [turn(tp)]

    def columns(tile):
        return pl.ds(pl.multiple_of(tile * TILE, TILE), TILE)

    def spectrum(part, block):
        return matmul(ahead[0, :, part], block) + matmul(ahead[1, :, part], block)

    def restore(places, real, imag):
        spec = jnp.concatenate([real, imag], axis=0)
        high = spec.astype(BF16)
        low = (spec - high.astype(F32)).astype(BF16)
        table = behind[0, places]
        return matmul(table, high) + matmul(behind[1, places], high) + matmul(table, low)

    @pl.loop(0, CHANNELS // TILE)
    def _(tile):
        cols = columns(tile)
        block = taps[cols]
        spec = matmul_nt(ahead[0, :, pl.ds(0, TAPS)], block)
        spec = spec + matmul_nt(ahead[1, :, pl.ds(0, TAPS)], block)
        tap_spec[pl.ds(0, HALF), cols] = spec[:HALF] + skip[:, cols]
        tap_spec[pl.ds(HALF, HALF), cols] = spec[HALF:]
        mixed_spec[:, cols] = spectrum(pl.ds(TAPS, ROWS), mixed[:, cols])

    right_top.wait_recv()
    forward_right = pass_cot(left, top, to_right)
    left_bottom.wait_recv()
    forward_left = pass_cot(right, bottom, to_left)

    to_near = place(y_near(y), z, core)
    near_copies, core_copies = [], []

    def share_import(number):
        imports[number].wait_recv()
        spot = weight_spot(1 - dp, taken_row, pieces[number])
        near_copies.append(send(spot, spot, to_near))
        core_copies.append(send(spot, spot, to_core))

    mixed_sent.wait_recv()

    @pl.loop(0, CHANNELS // TILE)
    def _(tile):
        cols = columns(tile)
        halo = jnp.where(seq > 0, mixed_halo[:, cols], jnp.zeros((TAPS, TILE), BF16))
        spec = mixed_spec[:, cols] + spectrum(pl.ds(0, TAPS), halo)
        real, imag = spec[:HALF], spec[HALF:]
        tap_real, tap_imag = tap_spec[pl.ds(0, HALF), cols], tap_spec[pl.ds(HALF, HALF), cols]
        value_now = restore(
            pl.ds(0, ROWS),
            real * tap_real - imag * tap_imag,
            real * tap_imag + imag * tap_real,
        )
        state[:, cols] = value_now
        gated[pl.ds(0, ROWS), cols] = (query[:, cols].astype(F32) * value_now).astype(BF16)

    gated_sent = send(gated.at[pl.ds(0, ROWS)], gated.at[pl.ds(ROWS, ROWS)], to_core)
    share_import(0)
    right_bottom.wait_recv()
    turns.append(turn(left))
    share_import(1)
    left_top.wait_recv()
    turns.append(turn(right))
    share_import(2)
    forward_right.wait_recv()
    forward_left.wait_recv()
    turns.append(turn(across))
    share_import(3)

    for copy in turns:
        copy.wait_recv()
    gated_sent.wait_recv()

    def exchange(quarter, step):
        axis, move = PLANS[quarter][step]
        there_y = move(y) if axis == "y" else y
        there_z = move(z) if axis == "z" else z
        landed = landing[quarter * 5 + step]
        return [
            send(slot_view(partial, quarter, slot), landed.at[i], place(there_y, there_z, core))
            for i, slot in enumerate(slots(PLANS[quarter], step, there_y, there_z))
        ]

    rounds = []
    for quarter in range(4):

        @pl.loop(0, 4)
        def _(part):
            rows = turned[pl.ds(part * 4, 4)].reshape(512, 2 * ROWS)
            block = matmul(rows, gated[:, pl.ds(quarter * TILE, TILE)]).astype(BF16)
            partial[
                quarter, lax.div(part, 2), pl.ds(lax.rem(part, 2) * 4, 4)
            ] = block.reshape(4, 2, 64, TILE)

        rounds.append(exchange(quarter, 0))

    def pass_near(number):
        near_copies[number].wait_recv()
        spot = weight_spot(1 - dp, near_row, pieces[number])
        core_copies.append(send(spot, spot, to_core))

    for number in range(4):
        pass_near(number)
    for copy in own:
        copy.wait()
    for copy in core_copies:
        copy.wait_recv()

    @pl.loop(0, CHANNELS // TILE)
    def _(tile):
        cols = columns(tile)
        total = matmul_nt(full_cot[0], full_weight[0, cols])
        for owner in range(1, 4):
            total = total + matmul_nt(full_cot[owner], full_weight[owner, cols])
        out_query[:, cols] = (total * state[:, cols]).astype(BF16)
        signal[:, cols] = (total * query[:, cols].astype(F32)).astype(BF16)

    signal_sent = send(signal.at[top], signal_halo, to_prior)

    def combine(quarter, step):
        for copy in rounds[quarter]:
            copy.wait_recv()
        landed = landing[quarter * 5 + step]
        for i, slot in enumerate(slots(PLANS[quarter], step, y, z)):
            view = slot_view(partial, quarter, slot)
            total = view[...].astype(F32) + landed[i].astype(F32)
            if step < 4:
                view[...] = total.astype(BF16)
            else:
                out_weight[:, pl.ds(quarter * TILE, TILE)] = total * scale
        if step < 4:
            rounds[quarter] = exchange(quarter, step + 1)

    for quarter in range(4):
        combine(quarter, 0)

    signal_sent.wait_recv()

    @pl.loop(0, CHANNELS // TILE)
    def _(tile):
        cols = columns(tile)
        halo = jnp.where(seq < 31, signal_halo[:, cols], jnp.zeros((TAPS, TILE), BF16))
        spec = spectrum(pl.ds(0, ROWS), signal[:, cols]) + spectrum(pl.ds(ROWS, TAPS), halo)
        real, imag = spec[:HALF], spec[HALF:]
        part_real, part_imag = mixed_spec[pl.ds(0, HALF), cols], mixed_spec[pl.ds(HALF, HALF), cols]
        lags = restore(
            pl.ds(2 * ROWS, TAPS),
            real * part_real + imag * part_imag,
            imag * part_real - real * part_imag,
        )
        for i in range(TILE // 128):
            block = lags[:, i * 128 : (i + 1) * 128].T
            lag_sum[tile * (TILE // 128) + i] = block.astype(BF16)
        tap_real, tap_imag = tap_spec[pl.ds(0, HALF), cols], tap_spec[pl.ds(HALF, HALF), cols]
        back = restore(
            pl.ds(ROWS, ROWS),
            real * tap_real + imag * tap_imag,
            imag * tap_real - real * tap_imag,
        )
        out_key[:, cols] = (back * value[:, cols].astype(F32)).astype(BF16)
        out_value[:, cols] = (back * key[:, cols].astype(F32)).astype(BF16)

    copies = [
        send(lag_sum.at[members[i]], near_land.at[i - 1], to_member(members[i])) for i in range(1, 8)
    ]
    for quarter in range(4):
        combine(quarter, 1)
    for copy in copies:
        copy.wait_recv()
    total = lag_sum[member].astype(F32)
    for i in range(7):
        total = total + near_land[i].astype(F32)
    lag_mid[...] = total.reshape(8, 16, TAPS)
    copies = [
        send(lag_mid.at[heights[i]], far_land.at[i - 1], place(y, heights[i], core))
        for i in range(1, 8)
    ]
    for quarter in range(4):
        combine(quarter, 2)
    for copy in copies:
        copy.wait_recv()
    total = lag_mid[z]
    for i in range(7):
        total = total + far_land[i]
    lag_out[member, z] = total * scale
    mine = lag_out.at[member, z]
    copies = [send(mine, mine, place(y, heights[i], core)) for i in range(1, 8)]
    for quarter in range(4):
        combine(quarter, 3)
    for copy in copies:
        copy.wait_recv()
    mine = lag_out.at[member]
    copies = [send(mine, mine, to_member(members[i])) for i in range(1, 8)]
    for quarter in range(4):
        combine(quarter, 4)
    for copy in copies:
        copy.wait_recv()
    out_filter[...] = lag_out[...]
    for copy in started:
        copy.wait_send()


def per_device(query_gate, key_gate, value_input, filter_taps, skip_gain, out_weight, cotangent):
    ahead, behind = spectrum_tables()
    vmem = pl.BlockSpec(memory_space=pltpu.VMEM)
    scratch = [
        ((4, ROWS, 1024), BF16),
        ((4, CHANNELS, 1024), BF16),
        ((16, 128, 2 * ROWS), BF16),
        ((16, 128, ROWS), BF16),
        ((2 * ROWS, CHANNELS), BF16),
        ((ROWS, CHANNELS), BF16),
        ((TAPS, CHANNELS), BF16),
        ((ROWS, CHANNELS), BF16),
        ((TAPS, CHANNELS), BF16),
        ((SIZE, CHANNELS), F32),
        ((SIZE, CHANNELS), F32),
        ((ROWS, CHANNELS), F32),
        ((8, 128), F32),
        ((4, 2, 8, 2, 64, TILE), BF16),
        ((8, 128, TAPS), BF16),
        ((8, 8, 16, TAPS), F32),
        ((7, 128, TAPS), BF16),
        ((8, 16, TAPS), F32),
        ((7, 16, TAPS), F32),
    ]
    grad_query, grad_key, grad_value, grad_filter, grad_weight = pl.pallas_call(
        kernel,
        out_shape=(
            jax.ShapeDtypeStruct((ROWS, CHANNELS), BF16),
            jax.ShapeDtypeStruct((ROWS, CHANNELS), BF16),
            jax.ShapeDtypeStruct((ROWS, CHANNELS), BF16),
            jax.ShapeDtypeStruct((8, 8, 16, TAPS), F32),
            jax.ShapeDtypeStruct((64, CHANNELS), F32),
        ),
        in_specs=[vmem] * 5 + [pl.BlockSpec(memory_space=pl.ANY)] + [vmem] * 3,
        out_specs=[vmem] * 5,
        scratch_shapes=[pltpu.VMEM(shape, dtype) for shape, dtype in scratch]
        + [
            pltpu.SemaphoreType.DMA((COPIES,)),
            pltpu.SemaphoreType.DMA((COPIES,)),
            pltpu.SemaphoreType.DMA((2,)),
        ]
        + [pltpu.VMEM(shape, BF16) for shape in landing_shapes()],
        compiler_params=pltpu.CompilerParams(
            collective_id=0, has_side_effects=True, vmem_limit_bytes=56 * 1024 * 1024
        ),
    )(
        query_gate[0], key_gate[0], value_input[0], filter_taps, skip_gain[None, :],
        out_weight, cotangent[0], jnp.asarray(ahead), jnp.asarray(behind),
    )
    grad_filter = grad_filter.reshape(CHANNELS, TAPS)
    return (
        grad_query[None],
        grad_key[None],
        grad_value[None],
        grad_filter,
        grad_filter[:, 0],
        grad_weight,
    )


def solution(mesh):
    return jax.shard_map(
        per_device,
        mesh=mesh,
        in_specs=(
            P("dp", "seq", "tp"),
            P("dp", "seq", "tp"),
            P("dp", "seq", "tp"),
            P("tp", None),
            P("tp"),
            P("tp", "dp"),
            P("dp", "seq", "tp"),
        ),
        out_specs=(
            P("dp", "seq", "tp"),
            P("dp", "seq", "tp"),
            P("dp", "seq", "tp"),
            P("tp", None),
            P("tp"),
            P(("seq", "dp"), "tp"),
        ),
        check_vma=False,
    )
```

```python
import itertools
import math

import jax
import jax.numpy as jnp
import ml_dtypes
import numpy as np
from jax import lax
from jax.experimental import pallas as pl
from jax.experimental.pallas import tpu as pltpu
from jax.sharding import PartitionSpec as P

ROWS = 256
TAPS = 128
SIZE = ROWS + TAPS
HALF = SIZE // 2
CHANNELS = 1024
TILE = 256
COPIES = 131
BF16 = jnp.bfloat16
F32 = jnp.float32


def split_table(table):
    high = table.astype(ml_dtypes.bfloat16)
    low = (table - high.astype(np.float64)).astype(ml_dtypes.bfloat16)
    return np.stack([high, low])


def spectrum_tables():
    odd = 2 * np.arange(HALF) + 1

    def angles(positions):
        return np.pi * ((odd[:, None] * positions[None, :]) % (2 * SIZE)) / SIZE

    ahead = angles(np.arange(SIZE))
    forward = np.concatenate([np.cos(ahead), -np.sin(ahead)], axis=0)
    places = np.concatenate(
        [np.arange(TAPS, SIZE), np.arange(ROWS), np.arange(-TAPS, 0)]
    )
    behind = angles(places).T
    inverse = (2.0 / SIZE) * np.concatenate([np.cos(behind), -np.sin(behind)], axis=1)
    return split_table(forward), split_table(inverse)


def matmul(left, right):
    return jnp.dot(left, right, preferred_element_type=F32)


def matmul_nt(left, right):
    return lax.dot_general(
        left, right, (((1,), (1,)), ((), ())), preferred_element_type=F32
    )


def y_near(y):
    return (1 - y[0], y[1])


def y_far(y):
    return (1 - y[0], 1 - y[1])


def z_up(z):
    return z + 1 - 2 * lax.rem(z, 2)


def z_down(z):
    return lax.rem(z + 2 * lax.rem(z, 2) + 7, 8)


def z_three(z):
    return lax.rem(z + 11 - 6 * lax.rem(z, 2), 8)


def z_back_three(z):
    return lax.rem(z + 5 + 6 * lax.rem(z, 2), 8)


PLANS = (
    (("y", y_near), ("y", y_far), ("z", z_up), ("z", z_down), ("z", z_three)),
    (("y", y_far), ("y", y_near), ("z", z_down), ("z", z_up), ("z", z_back_three)),
    (("z", z_up), ("z", z_down), ("y", y_near), ("y", y_far), ("z", z_three)),
    (("z", z_down), ("z", z_up), ("y", y_far), ("y", y_near), ("z", z_back_three)),
)


def kept(rest, place):
    if not rest:
        return [place]
    return kept(rest[1:], place) + kept(rest[1:], rest[0](place))


def remaining(plan, step, axis):
    return [move for name, move in plan[step + 1 :] if name == axis]


def slots(plan, step, y, z):
    y_rest, z_rest = remaining(plan, step, "y"), remaining(plan, step, "z")
    y_list = [None] if len(y_rest) == 2 else kept(y_rest, y)
    z_list = [None] if len(z_rest) == 3 else kept(z_rest, z)
    return [(one, other) for one in y_list for other in z_list]


def slot_view(ref, quarter, slot):
    y, z = slot
    if y is None:
        return ref.at[quarter, :, z]
    if z is None:
        return ref.at[quarter, y[0], :, y[1]]
    return ref.at[quarter, y[0], z, y[1]]


def landing_shapes():
    shapes = []
    for plan in PLANS:
        for step in range(5):
            y_rest, z_rest = remaining(plan, step, "y"), remaining(plan, step, "z")
            if step == 0:
                shape = (4, 4, 64, TILE) if plan[0][0] == "y" else (4, 2, 2, 64, TILE)
            elif len(y_rest) == 2:
                shape = (2 ** len(z_rest), 2, 2, 64, TILE)
            elif len(z_rest) == 3:
                shape = (2 ** len(y_rest), 8, 64, TILE)
            else:
                shape = (2 ** (len(y_rest) + len(z_rest)), 64, TILE)
            shapes.append(shape)
    return shapes


def first_slots(quarter, owner, y, z, keep):
    low, half = lax.div(owner, 2), lax.rem(owner, 2)
    group = pl.ds(half * 4, 4)
    other = 0 if keep else 1
    if quarter == 0:
        return [(low, group, lax.rem(y[1] + y[0] + low + other, 2))]
    if quarter == 1:
        return [(low, group, lax.rem(y[1] + other, 2))]
    if quarter == 2:
        kind = lax.rem(lax.div(lax.rem(z, 4) + 1, 2) + other, 2)
        return [(low, half * 4 + kind + i * (3 - 2 * kind)) for i in range(2)]
    kind = lax.rem(lax.div(lax.rem(z, 4), 2) + other, 2)
    return [(low, half * 4 + kind * 2 + i) for i in range(2)]


def kernel(
    query_in, key_in, value_in, taps_in, skip_in, weight, cot, ahead_in, behind_in,
    query_out, key_out, value_out, filter_out, skip_out, weight_out,
    query, key, value, taps, skip, ahead, behind,
    full_cot, full_weight, turned, turned_away, gated, mixed, mixed_halo, signal, signal_halo,
    tap_spec, mixed_spec, signal_spec, state, grad_gated, partial, lag_sum, lag_out,
    near_land, lag_mid, far_land, lag_last, made_query, made_key, made_value, made_filter,
    made_skip, made_weight, send_sem, recv_sem, local_sem, *landing,
):
    seq, tp, dp = lax.axis_index("seq"), lax.axis_index("tp"), lax.axis_index("dp")
    core = lax.rem(seq, 2)
    z = lax.rem(lax.div(seq, 2), 8)
    y = (lax.div(seq, 16), dp)
    scale = 1.0 / math.sqrt(2 * 32 * ROWS)

    def place(y, z, core):
        return ((y[0] * 8 + z) * 2 + core, tp, y[1])

    right, left, across = lax.rem(tp + 1, 4), lax.rem(tp + 3, 4), lax.rem(tp + 2, 4)
    to_right, to_left = (seq, right, dp), (seq, left, dp)
    to_next, to_prior = (lax.rem(seq + 1, 32), tp, dp), (lax.rem(seq + 31, 32), tp, dp)
    to_core = place(y, z, 1 - core)
    to_near, to_far = place(y_near(y), z, core), place(y_far(y), z, core)
    to_side = [place(y, z_up(z), core), place(y, z_down(z), core)]
    member = (y[1] * 2 + y[0]) * 2 + core

    def to_member(index):
        high = lax.div(index, 4)
        return place((lax.rem(lax.div(index, 2), 2), high), z, lax.rem(index, 2))

    members = [lax.rem(member + i, 8) for i in range(8)]
    heights = [lax.rem(z + i, 8) for i in range(8)]

    barrier = pltpu.get_barrier_semaphore()
    greeted = [to_right, to_left, to_next, to_prior]
    greeted += [to_member(members[i]) for i in range(1, 8)]
    greeted += [place(y, heights[i], core) for i in range(1, 8)]
    for target in greeted:
        pl.semaphore_signal(
            barrier, inc=1, device_id=target, device_id_type=pl.DeviceIdType.MESH
        )

    local_numbers = itertools.count()

    def fetch(source, target):
        copy = pltpu.make_async_copy(source, target, local_sem.at[next(local_numbers)])
        copy.start()
        return copy

    key_copy, value_copy = fetch(key_in, key), fetch(value_in, value)
    cot_copy = fetch(cot, full_cot.at[tp])
    table_copies = [fetch(ahead_in, ahead), fetch(taps_in, taps), fetch(skip_in, skip)]
    state_copies = [fetch(behind_in, behind), fetch(query_in, query)]
    pl.semaphore_wait(barrier, len(greeted))

    numbers = itertools.count()
    started = []

    def send(source, target_ref, target):
        number = next(numbers)
        copy = pltpu.make_async_remote_copy(
            src_ref=source,
            dst_ref=target_ref,
            send_sem=send_sem.at[number],
            recv_sem=recv_sem.at[number],
            device_id=target,
            device_id_type=pl.DeviceIdType.MESH,
        )
        copy.start()
        started.append(copy)
        return copy

    top, bottom = pl.ds(0, 128), pl.ds(128, 128)

    def pass_cot(owner, part, target):
        spot = full_cot.at[owner, part]
        return send(spot, spot, target)

    right_top = send(cot.at[top], full_cot.at[tp, top], to_right)
    left_bottom = send(cot.at[bottom], full_cot.at[tp, bottom], to_left)

    def weight_rows(low, odd, core):
        return pl.ds(pl.multiple_of(((low * 2 + odd) * 2 + core) * 128, 128), 128)

    odd = lax.rem(z, 2)
    given = weight_rows(1 - y[0], odd, core)
    imports = []
    for i in range(2):
        for r in range(2):
            rows = pl.ds(pl.multiple_of(given.start + r * 64, 64), 64)
            source = weight.at[rows, pl.ds(i * 1024, 1024)]
            imports.append(send(source, full_weight.at[dp * 2 + i, rows], to_far))
    right_bottom = send(cot.at[bottom], full_cot.at[tp, bottom], to_right)
    left_top = send(cot.at[top], full_cot.at[tp, top], to_left)
    own = [fetch(weight.at[:, pl.ds(i * 1024, 1024)], full_weight.at[dp * 2 + i]) for i in range(2)]

    key_copy.wait()
    value_copy.wait()
    mixed[...] = (key[...].astype(F32) * value[...].astype(F32)).astype(BF16)
    mixed_sent = send(mixed.at[bottom], mixed_halo, to_next)

    def turn(owner):
        for i in range(4):
            mine = pl.ds(pl.multiple_of((i * 2 + core) * 128, 128), 128)
            other = pl.ds(pl.multiple_of((i * 2 + 1 - core) * 128, 128), 128)
            turned[owner * 4 + i, :, pl.ds(0, ROWS)] = full_cot[owner, :, mine].T
            turned_away[owner * 4 + i] = full_cot[owner, :, other].T
        group = pl.ds(owner * 4, 4)
        return send(turned_away.at[group], turned.at[group, :, pl.ds(ROWS, ROWS)], to_core)

    cot_copy.wait()
    turned_own = turn(tp)

    def columns(tile):
        return pl.ds(pl.multiple_of(tile * TILE, TILE), TILE)

    def spectrum(part, block):
        return matmul(ahead[0, :, part], block) + matmul(ahead[1, :, part], block)

    def restore(places, real, imag):
        spec = jnp.concatenate([real, imag], axis=0)
        high = spec.astype(BF16)
        low = (spec - high.astype(F32)).astype(BF16)
        table = behind[0, places]
        return matmul(table, high) + matmul(behind[1, places], high) + matmul(table, low)

    for copy in table_copies:
        copy.wait()

    @pl.loop(0, CHANNELS // TILE)
    def _(tile):
        cols = columns(tile)
        block = taps[cols]
        spec = matmul_nt(ahead[0, :, pl.ds(0, TAPS)], block)
        spec = spec + matmul_nt(ahead[1, :, pl.ds(0, TAPS)], block)
        tap_spec[pl.ds(0, HALF), cols] = spec[:HALF] + skip[:, cols]
        tap_spec[pl.ds(HALF, HALF), cols] = spec[HALF:]
        mixed_spec[:, cols] = spectrum(pl.ds(TAPS, ROWS), mixed[:, cols])

    for copy in state_copies:
        copy.wait()
    mixed_sent.wait_recv()

    @pl.loop(0, CHANNELS // TILE)
    def _(tile):
        cols = columns(tile)
        halo = jnp.where(seq > 0, mixed_halo[:, cols], jnp.zeros((TAPS, TILE), BF16))
        spec = mixed_spec[:, cols] + spectrum(pl.ds(0, TAPS), halo)
        mixed_spec[:, cols] = spec
        real, imag = spec[:HALF], spec[HALF:]
        tap_real, tap_imag = tap_spec[pl.ds(0, HALF), cols], tap_spec[pl.ds(HALF, HALF), cols]
        value_now = restore(
            pl.ds(0, ROWS),
            real * tap_real - imag * tap_imag,
            real * tap_imag + imag * tap_real,
        )
        state[:, cols] = value_now
        gated[pl.ds(0, ROWS), cols] = (query[:, cols].astype(F32) * value_now).astype(BF16)

    gated_sent = send(gated.at[pl.ds(0, ROWS)], gated.at[pl.ds(ROWS, ROWS)], to_core)

    right_top.wait_recv()
    forward_right = pass_cot(left, top, to_right)
    left_bottom.wait_recv()
    forward_left = pass_cot(right, bottom, to_left)

    near_copies, side_copies, corner_copies, core_copies = [], [], [], []
    here, beside = weight_rows(y[0], odd, core), weight_rows(1 - y[0], odd, core)
    above, corner = weight_rows(y[0], 1 - odd, core), weight_rows(1 - y[0], 1 - odd, core)

    def weight_spot(rows, number):
        part = pl.ds(pl.multiple_of(rows.start + number % 2 * 64, 64), 64)
        return full_weight.at[(1 - dp) * 2 + number // 2, part]

    def share_import(number):
        imports[number].wait_recv()
        spot = weight_spot(here, number)
        near_copies.append(send(spot, spot, to_near))
        side_copies.append(send(spot, spot, to_side[number % 2]))
        core_copies.append(send(spot, spot, to_core))

    def share_near(number):
        near_copies[number].wait_recv()
        spot = weight_spot(beside, number)
        corner_copies.append(send(spot, spot, to_side[number % 2]))
        core_copies.append(send(spot, spot, to_core))

    def share_last(copy, rows, number):
        copy.wait_recv()
        spot = weight_spot(rows, number)
        core_copies.append(send(spot, spot, to_core))

    first = [[] for _ in range(4)]

    def first_view(ref, quarter, slot):
        if quarter < 2:
            return ref.at[quarter, slot[0], slot[1], slot[2]]
        return ref.at[quarter, slot[0], slot[1]]

    def first_landing(quarter, chunk, i):
        return landing[quarter * 5].at[chunk] if quarter < 2 else landing[quarter * 5].at[chunk, i]

    first_targets = [to_near, to_far, to_side[0], to_side[1]]

    def products(chunk, owner):
        low, group = lax.div(owner, 2), pl.ds(lax.rem(owner, 2) * 4, 4)

        @pl.loop(0, 4)
        def _(quarter):
            rows = turned[pl.ds(owner * 4, 4)].reshape(512, 2 * ROWS)
            block = matmul(rows, gated[:, columns(quarter)]).astype(BF16)
            partial[quarter, low, group] = block.reshape(4, 2, 64, TILE)

    def halve(chunk, owner, quarters):
        for quarter in quarters:
            for i, slot in enumerate(first_slots(quarter, owner, y, z, False)):
                first[quarter].append(
                    send(
                        first_view(partial, quarter, slot),
                        first_landing(quarter, chunk, i),
                        first_targets[quarter],
                    )
                )

    share_import(0)
    share_import(1)
    turned_own.wait_recv()
    gated_sent.wait_recv()
    products(0, tp)
    halve(0, tp, (1,))
    share_import(2)
    share_import(3)
    share_near(0)
    share_near(1)
    right_bottom.wait_recv()
    turned_left = turn(left)
    left_top.wait_recv()
    turned_right = turn(right)
    turned_left.wait_recv()
    products(1, left)
    halve(1, left, (1,))
    share_near(2)
    share_near(3)
    halve(0, tp, (0, 2, 3))
    halve(1, left, (0, 2, 3))
    turned_right.wait_recv()
    products(2, right)
    halve(2, right, (0, 1, 2, 3))
    forward_right.wait_recv()
    forward_left.wait_recv()
    turned_across = turn(across)
    for copy in own:
        copy.wait()

    @pl.loop(0, CHANNELS // TILE)
    def _(tile):
        cols = columns(tile)
        total = matmul_nt(full_cot[dp * 2], full_weight[dp * 2, cols])
        grad_gated[:, cols] = total + matmul_nt(full_cot[dp * 2 + 1], full_weight[dp * 2 + 1, cols])

    turned_across.wait_recv()
    products(3, across)
    halve(3, across, (0, 1, 2, 3))
    for number in range(4):
        share_last(side_copies[number], above, number)
    for number in range(4):
        share_last(corner_copies[number], corner, number)
    for copy in core_copies:
        copy.wait_recv()

    @pl.loop(0, CHANNELS // TILE)
    def _(tile):
        cols = columns(tile)
        total = grad_gated[:, cols]
        for i in range(2):
            owner = (1 - dp) * 2 + i
            total = total + matmul_nt(full_cot[owner], full_weight[owner, cols])
        made_query[:, cols] = (total * state[:, cols]).astype(BF16)
        signal[:, cols] = (total * query[:, cols].astype(F32)).astype(BF16)

    signal_sent = send(signal.at[top], signal_halo, to_prior)
    outgoing = [fetch(made_query, query_out)]

    @pl.loop(0, CHANNELS // TILE)
    def _(tile):
        cols = columns(tile)
        spec = spectrum(pl.ds(0, ROWS), signal[:, cols])
        signal_spec[:, cols] = spec
        real, imag = spec[:HALF], spec[HALF:]
        part_real, part_imag = mixed_spec[pl.ds(0, HALF), cols], mixed_spec[pl.ds(HALF, HALF), cols]
        lags = restore(
            pl.ds(2 * ROWS, TAPS),
            real * part_real + imag * part_imag,
            imag * part_real - real * part_imag,
        )
        for i in range(TILE // 128):
            block = lags[:, i * 128 : (i + 1) * 128].T
            lag_sum[tile * (TILE // 128) + i] = block.astype(BF16)

    copies = [
        send(lag_sum.at[members[i]], near_land.at[i - 1], to_member(members[i])) for i in range(1, 8)
    ]

    rounds = [None] * 4

    def exchange(quarter, step):
        axis, move = PLANS[quarter][step]
        there_y = move(y) if axis == "y" else y
        there_z = move(z) if axis == "z" else z
        landed = landing[quarter * 5 + step]
        rounds[quarter] = [
            send(slot_view(partial, quarter, slot), landed.at[i], place(there_y, there_z, core))
            for i, slot in enumerate(slots(PLANS[quarter], step, there_y, there_z))
        ]

    def combine(quarter, step):
        if step == 0:
            for copy in first[quarter]:
                copy.wait_recv()
            pairs = [
                (first_view(partial, quarter, slot), first_landing(quarter, chunk, i))
                for chunk, owner in enumerate((tp, left, right, across))
                for i, slot in enumerate(first_slots(quarter, owner, y, z, True))
            ]
        else:
            for copy in rounds[quarter]:
                copy.wait_recv()
            landed = landing[quarter * 5 + step]
            pairs = [
                (slot_view(partial, quarter, slot), landed.at[i])
                for i, slot in enumerate(slots(PLANS[quarter], step, y, z))
            ]
        for view, landed in pairs:
            total = view[...].astype(F32) + landed[...].astype(F32)
            if step < 4:
                view[...] = total.astype(BF16)
            else:
                made_weight[:, pl.ds(quarter * TILE, TILE)] = total * scale
        if step < 4:
            exchange(quarter, step + 1)

    for quarter in range(4):
        combine(quarter, 0)

    signal_sent.wait_recv()

    @pl.loop(0, CHANNELS // TILE)
    def _(tile):
        cols = columns(tile)
        halo = jnp.where(seq < 31, signal_halo[:, cols], jnp.zeros((TAPS, TILE), BF16))
        spec = signal_spec[:, cols] + spectrum(pl.ds(ROWS, TAPS), halo)
        real, imag = spec[:HALF], spec[HALF:]
        tap_real, tap_imag = tap_spec[pl.ds(0, HALF), cols], tap_spec[pl.ds(HALF, HALF), cols]
        back = restore(
            pl.ds(ROWS, ROWS),
            real * tap_real + imag * tap_imag,
            imag * tap_real - real * tap_imag,
        )
        made_key[:, cols] = (back * value[:, cols].astype(F32)).astype(BF16)
        made_value[:, cols] = (back * key[:, cols].astype(F32)).astype(BF16)

    outgoing += [fetch(made_key, key_out), fetch(made_value, value_out)]

    for copy in copies:
        copy.wait_recv()
    total = lag_sum[member].astype(F32)
    for i in range(7):
        total = total + near_land[i].astype(F32)
    lag_mid[...] = total.reshape(8, 16, TAPS)
    copies = [
        send(lag_mid.at[heights[i]], far_land.at[i - 1], place(y, heights[i], core))
        for i in range(1, 8)
    ]
    for quarter in range(4):
        combine(quarter, 1)
    for copy in copies:
        copy.wait_recv()
    total = lag_mid[z]
    for i in range(7):
        total = total + far_land[i]
    lag_out[member, z] = (total * scale).astype(BF16)
    mine = lag_out.at[member, z]
    copies = [send(mine, mine, place(y, heights[i], core)) for i in range(1, 8)]
    for quarter in range(4):
        combine(quarter, 2)
    for copy in copies:
        copy.wait_recv()
    mine = lag_out.at[member]
    copies = [send(mine, mine, to_member(members[i])) for i in range(1, 8)]
    for quarter in range(4):
        combine(quarter, 3)
    for copy in copies:
        copy.wait_recv()
    made_filter[...] = lag_out[...].astype(F32)
    outgoing.append(fetch(made_filter, filter_out))
    diagonal = lax.broadcasted_iota(jnp.int32, (128, 128), 0) == lax.broadcasted_iota(
        jnp.int32, (128, 128), 1
    )
    for i in range(8):
        first_lag = made_filter[i].reshape(128, TAPS)[:, 0:1]
        spread = jnp.where(diagonal, jnp.broadcast_to(first_lag, (128, 128)), 0.0)
        made_skip[pl.ds(i, 1)] = jnp.sum(spread, axis=0, keepdims=True)
    outgoing.append(fetch(made_skip, skip_out))
    for quarter in range(4):
        combine(quarter, 4)
    outgoing.append(fetch(made_weight, weight_out))
    for copy in started:
        copy.wait_send()
    for copy in outgoing:
        copy.wait()


def hand_on(*refs):
    count = (len(refs) - 2) // 3
    sources, targets, held = refs[:count], refs[count : 2 * count], refs[2 * count : 3 * count]
    in_sem, out_sem = refs[-2:]
    loads = [pltpu.make_async_copy(sources[i], held[i], in_sem.at[i]) for i in range(count)]
    stores = [pltpu.make_async_copy(held[i], targets[i], out_sem.at[i]) for i in range(count)]
    for copy in loads:
        copy.start()
    for load, store in zip(loads, stores):
        load.wait()
        store.start()
    for copy in stores:
        copy.wait()


def per_device(query_gate, key_gate, value_input, filter_taps, skip_gain, out_weight, cotangent):
    ahead, behind = spectrum_tables()
    anywhere = pl.BlockSpec(memory_space=pl.ANY)
    block = ((ROWS, CHANNELS), BF16)
    scratch = [
        block,
        block,
        block,
        ((CHANNELS, TAPS), BF16),
        ((1, CHANNELS), F32),
        (ahead.shape, BF16),
        (behind.shape, BF16),
        ((4, ROWS, 1024), BF16),
        ((4, CHANNELS, 1024), BF16),
        ((16, 128, 2 * ROWS), BF16),
        ((16, 128, ROWS), BF16),
        ((2 * ROWS, CHANNELS), BF16),
        block,
        ((TAPS, CHANNELS), BF16),
        block,
        ((TAPS, CHANNELS), BF16),
        ((SIZE, CHANNELS), F32),
        ((SIZE, CHANNELS), F32),
        ((SIZE, CHANNELS), F32),
        ((ROWS, CHANNELS), F32),
        ((ROWS, CHANNELS), F32),
        ((4, 2, 8, 2, 64, TILE), BF16),
        ((8, 128, TAPS), BF16),
        ((8, 8, 16, TAPS), BF16),
        ((7, 128, TAPS), BF16),
        ((8, 16, TAPS), F32),
        ((7, 16, TAPS), F32),
        ((8, 128), F32),
        block,
        block,
        block,
        ((8, 8, 16, TAPS), F32),
        ((8, 128), F32),
        ((64, CHANNELS), F32),
    ]
    results = pl.pallas_call(
        kernel,
        out_shape=(
            jax.ShapeDtypeStruct((ROWS, CHANNELS), BF16),
            jax.ShapeDtypeStruct((ROWS, CHANNELS), BF16),
            jax.ShapeDtypeStruct((ROWS, CHANNELS), BF16),
            jax.ShapeDtypeStruct((8, 8, 16, TAPS), F32),
            jax.ShapeDtypeStruct((8, 128), F32),
            jax.ShapeDtypeStruct((64, CHANNELS), F32),
        ),
        in_specs=[anywhere] * 9,
        out_specs=[anywhere] * 6,
        scratch_shapes=[pltpu.VMEM(shape, dtype) for shape, dtype in scratch]
        + [
            pltpu.SemaphoreType.DMA((COPIES,)),
            pltpu.SemaphoreType.DMA((COPIES,)),
            pltpu.SemaphoreType.DMA((16,)),
        ]
        + [pltpu.VMEM(shape, BF16) for shape in landing_shapes()],
        compiler_params=pltpu.CompilerParams(
            collective_id=0, has_side_effects=True, vmem_limit_bytes=56 * 1024 * 1024
        ),
    )(
        query_gate[0], key_gate[0], value_input[0], filter_taps, skip_gain[None, :],
        out_weight, cotangent[0], jnp.asarray(ahead), jnp.asarray(behind),
    )
    results = [
        results[0][None],
        results[1][None],
        results[2][None],
        results[3].reshape(CHANNELS, TAPS),
        results[4].reshape(CHANNELS),
        results[5],
    ]
    return tuple(
        pl.pallas_call(
            hand_on,
            out_shape=[jax.ShapeDtypeStruct(x.shape, x.dtype) for x in results],
            in_specs=[anywhere] * 6,
            out_specs=[anywhere] * 6,
            scratch_shapes=[pltpu.VMEM(x.shape, x.dtype) for x in results]
            + [pltpu.SemaphoreType.DMA((6,))] * 2,
        )(*results)
    )


def solution(mesh):
    return jax.shard_map(
        per_device,
        mesh=mesh,
        in_specs=(
            P("dp", "seq", "tp"),
            P("dp", "seq", "tp"),
            P("dp", "seq", "tp"),
            P("tp", None),
            P("tp"),
            P("tp", "dp"),
            P("dp", "seq", "tp"),
        ),
        out_specs=(
            P("dp", "seq", "tp"),
            P("dp", "seq", "tp"),
            P("dp", "seq", "tp"),
            P("tp", None),
            P("tp"),
            P(("seq", "dp"), "tp"),
        ),
        check_vma=False,
    )
```

```python
import itertools
import math

import jax
import jax.numpy as jnp
import ml_dtypes
import numpy as np
from jax import lax
from jax.experimental import pallas as pl
from jax.experimental.pallas import tpu as pltpu
from jax.sharding import PartitionSpec as P

ROWS = 256
TAPS = 128
SIZE = ROWS + TAPS
HALF = SIZE // 2
CHANNELS = 1024
TILE = 256
STREAMS = 2
LANES = TILE // STREAMS
PER_QUARTER = 5 * STREAMS
SENT_ROWS = 2048
OUT_EXTRA, OUT_SETS = 4, 3
COPIES = 94
BF16 = jnp.bfloat16
F32 = jnp.float32


PARTS = ((TAPS, ROWS), (0, TAPS), (0, ROWS), (ROWS, TAPS))
LATE_BLOCK, EARLY_HALO, EARLY_BLOCK, LATE_HALO = 0, 2 * ROWS, 2 * SIZE, 2 * SIZE + 2 * ROWS


def split_table(table):
    high = table.astype(ml_dtypes.bfloat16)
    return high, (table - high.astype(np.float64)).astype(ml_dtypes.bfloat16)


def spectrum_tables():
    odd = 2 * np.arange(HALF) + 1

    def angles(positions):
        return np.pi * ((odd[:, None] * positions[None, :]) % (2 * SIZE)) / SIZE

    ahead = angles(np.arange(SIZE))
    forward = np.concatenate([np.cos(ahead), -np.sin(ahead)], axis=0)
    places = np.concatenate(
        [np.arange(TAPS, SIZE), np.arange(ROWS), np.arange(-TAPS, 0)]
    )
    behind = angles(places).T
    inverse = (2.0 / SIZE) * np.concatenate([np.cos(behind), -np.sin(behind)], axis=1)
    high, low = split_table(forward)
    pieces = [piece[:, start : start + size] for start, size in PARTS for piece in (high, low)]
    back_high, back_low = split_table(inverse)
    return (
        np.concatenate(pieces, axis=1),
        np.concatenate([back_high, back_low, back_high], axis=1),
    )


def matmul(left, right):
    return jnp.dot(left, right, preferred_element_type=F32)


def matmul_nt(left, right):
    return lax.dot_general(
        left, right, (((1,), (1,)), ((), ())), preferred_element_type=F32
    )


def y_near(y):
    return (1 - y[0], y[1])


def y_far(y):
    return (1 - y[0], 1 - y[1])


def z_up(z):
    return z + 1 - 2 * lax.rem(z, 2)


def z_down(z):
    return lax.rem(z + 2 * lax.rem(z, 2) + 7, 8)


def z_three(z):
    return lax.rem(z + 11 - 6 * lax.rem(z, 2), 8)


def z_back_three(z):
    return lax.rem(z + 5 + 6 * lax.rem(z, 2), 8)


PLANS = (
    (("y", y_near), ("y", y_far), ("z", z_up), ("z", z_down), ("z", z_three)),
    (("y", y_far), ("y", y_near), ("z", z_down), ("z", z_up), ("z", z_back_three)),
    (("z", z_up), ("z", z_down), ("y", y_near), ("y", y_far), ("z", z_three)),
    (("z", z_down), ("z", z_up), ("y", y_far), ("y", y_near), ("z", z_back_three)),
)


def kept(rest, place):
    if not rest:
        return [place]
    return kept(rest[1:], place) + kept(rest[1:], rest[0](place))


def remaining(plan, step, axis):
    return [move for name, move in plan[step + 1 :] if name == axis]


def slots(plan, step, y, z):
    y_rest, z_rest = remaining(plan, step, "y"), remaining(plan, step, "z")
    y_list = [None] if len(y_rest) == 2 else kept(y_rest, y)
    z_list = [None] if len(z_rest) == 3 else kept(z_rest, z)
    return [(one, other) for one in y_list for other in z_list]


def slot_view(ref, quarter, slot, lanes):
    y, z = slot
    if y is None:
        return ref.at[quarter, :, z, :, :, lanes]
    if z is None:
        return ref.at[quarter, y[0], :, y[1], :, lanes]
    return ref.at[quarter, y[0], z, y[1], :, lanes]


def planes_of(size):
    for planes in range(1, 5):
        if size % (2048 * 16 * planes) == 0 and size // (2048 * planes) <= 1024:
            return planes
    return None


def landing_shapes():
    shapes = []
    for plan in PLANS:
        shapes += [(4, 4, 64, LANES) if plan[0][0] == "y" else (4, 2, 2, 64, LANES)] * STREAMS
        for step in range(1, 5):
            y_rest, z_rest = remaining(plan, step, "y"), remaining(plan, step, "z")
            if len(y_rest) == 2:
                shape = (2 ** len(z_rest), 2, 2, 64, LANES)
            elif len(z_rest) == 3:
                shape = (2 ** len(y_rest), 8, 64, LANES)
            else:
                shape = (2 ** (len(y_rest) + len(z_rest)), 64, LANES)
            shapes += [shape] * STREAMS
    return shapes


def first_slots(quarter, owner, y, z, keep):
    low, half = lax.div(owner, 2), lax.rem(owner, 2)
    group = pl.ds(half * 4, 4)
    other = 0 if keep else 1
    if quarter == 0:
        return [(low, group, lax.rem(y[1] + y[0] + low + other, 2))]
    if quarter == 1:
        return [(low, group, lax.rem(y[1] + other, 2))]
    if quarter == 2:
        kind = lax.rem(lax.div(lax.rem(z, 4) + 1, 2) + other, 2)
        return [(low, half * 4 + kind + i * (3 - 2 * kind)) for i in range(2)]
    kind = lax.rem(lax.div(lax.rem(z, 4), 2) + other, 2)
    return [(low, half * 4 + kind * 2 + i) for i in range(2)]


def kernel(
    query_in, key_in, value_in, taps_in, skip_in, weight, cot, ahead_in, behind_in,
    made_query, made_key, made_value, made_filter, made_skip, made_weight,
    query, key, value, taps, skip, ahead, behind,
    full_cot, full_weight, turned, turned_away, gated, mixed, mixed_halo, signal, signal_halo,
    tap_spec, mixed_spec, signal_spec, state, grad_gated, partial, lag_sum, lag_out,
    near_land, lag_mid, far_land, send_sem, recv_sem, local_sem, *landing,
):
    seq, tp, dp = lax.axis_index("seq"), lax.axis_index("tp"), lax.axis_index("dp")
    core = lax.rem(seq, 2)
    z = lax.rem(lax.div(seq, 2), 8)
    y = (lax.div(seq, 16), dp)
    scale = 1.0 / math.sqrt(2 * 32 * ROWS)

    def place(y, z, core):
        return ((y[0] * 8 + z) * 2 + core, tp, y[1])

    right, left, across = lax.rem(tp + 1, 4), lax.rem(tp + 3, 4), lax.rem(tp + 2, 4)
    to_right, to_left = (seq, right, dp), (seq, left, dp)
    to_next, to_prior = (lax.rem(seq + 1, 32), tp, dp), (lax.rem(seq + 31, 32), tp, dp)
    to_core = place(y, z, 1 - core)
    to_near, to_far = place(y_near(y), z, core), place(y_far(y), z, core)
    to_side = [place(y, z_up(z), core), place(y, z_down(z), core)]
    member = (y[1] * 2 + y[0]) * 2 + core

    def to_member(index):
        high = lax.div(index, 4)
        return place((lax.rem(lax.div(index, 2), 2), high), z, lax.rem(index, 2))

    members = [lax.rem(member + i, 8) for i in range(8)]
    heights = [lax.rem(z + i, 8) for i in range(8)]

    barrier = pltpu.get_barrier_semaphore()
    greeted = [to_right, to_left, to_next, to_prior]
    greeted += [to_member(members[i]) for i in range(1, 8)]
    greeted += [place(y, heights[i], core) for i in range(1, 8)]
    for target in greeted:
        pl.semaphore_signal(
            barrier, inc=1, device_id=target, device_id_type=pl.DeviceIdType.MESH
        )

    local_numbers = itertools.count()

    def fetch(source, target):
        copy = pltpu.make_async_copy(source, target, local_sem.at[next(local_numbers)])
        copy.start()
        return copy

    key_copy, value_copy = fetch(key_in, key), fetch(value_in, value)
    cot_copy = fetch(cot, full_cot.at[tp])
    table_copies = [fetch(ahead_in, ahead), fetch(taps_in, taps), fetch(skip_in, skip)]
    state_copies = [fetch(behind_in, behind), fetch(query_in, query)]
    pl.semaphore_wait(barrier, len(greeted))

    numbers = itertools.count()
    started = []

    def describe(source, target_ref, target, number, out_number):
        return pltpu.make_async_remote_copy(
            src_ref=source,
            dst_ref=target_ref,
            send_sem=send_sem.at[out_number],
            recv_sem=recv_sem.at[number],
            device_id=target,
            device_id_type=pl.DeviceIdType.MESH,
        )

    def send(source, target_ref, target, group=None, out=None):
        size = math.prod(source.shape) * source.dtype.itemsize
        if out is None:
            if not started or started[-1] >= SENT_ROWS * 2048 and planes_of(started[-1]):
                started.append(0)
            started[-1] += size
        number = next(numbers) if group is None else group[1]
        out_number = OUT_EXTRA + len(started) - 1 if out is None else out
        copy = describe(source, target_ref, target, number, out_number)
        copy.start()
        return copy

    def gather(landed):
        number = next(numbers)
        return describe(landed, landed, to_core, number, 0), number

    top, bottom = pl.ds(0, 128), pl.ds(128, 128)

    def pass_cot(owner, part, target):
        spot = full_cot.at[owner, part]
        return send(spot, spot, target)

    right_top = send(cot.at[top], full_cot.at[tp, top], to_right)
    left_bottom = send(cot.at[bottom], full_cot.at[tp, bottom], to_left)

    def weight_rows(low, odd, core):
        return pl.ds(pl.multiple_of(((low * 2 + odd) * 2 + core) * 128, 128), 128)

    odd = lax.rem(z, 2)
    given = weight_rows(1 - y[0], odd, core)
    imports = []
    for i in range(2):
        for r in range(4):
            rows = pl.ds(pl.multiple_of(given.start + r * 32, 32), 32)
            source = weight.at[rows, pl.ds(i * 1024, 1024)]
            imports.append(send(source, full_weight.at[dp * 2 + i, rows], to_far))
    right_bottom = send(cot.at[bottom], full_cot.at[tp, bottom], to_right)
    left_top = send(cot.at[top], full_cot.at[tp, top], to_left)
    own = [fetch(weight.at[:, pl.ds(i * 1024, 1024)], full_weight.at[dp * 2 + i]) for i in range(2)]

    key_copy.wait()
    value_copy.wait()
    mixed[...] = (key[...].astype(F32) * value[...].astype(F32)).astype(BF16)
    mixed_sent = send(mixed.at[bottom], mixed_halo, to_next)

    def turn(owner, start, size):
        tokens, far_tokens = pl.ds(start, size), pl.ds(ROWS + start, size)
        for i in range(4):
            mine = pl.ds(pl.multiple_of((i * 2 + core) * 128, 128), 128)
            other = pl.ds(pl.multiple_of((i * 2 + 1 - core) * 128, 128), 128)
            turned[owner * 4 + i, :, tokens] = full_cot[owner, tokens, mine].T
            turned_away[owner * 4 + i, :, tokens] = full_cot[owner, tokens, other].T
        group = pl.ds(owner * 4, 4)
        return send(turned_away.at[group, :, tokens], turned.at[group, :, far_tokens], to_core)

    cot_copy.wait()
    turned_own = turn(tp, 0, ROWS)

    def columns(tile):
        return pl.ds(pl.multiple_of(tile * TILE, TILE), TILE)

    def spectrum(start, block):
        table = ahead[:, pl.ds(start, 2 * block.shape[0])]
        return matmul(table, jnp.concatenate([block, block], axis=0))

    def restore(places, real, imag):
        spec = jnp.concatenate([real, imag], axis=0)
        high = spec.astype(BF16)
        low = (spec - high.astype(F32)).astype(BF16)
        return matmul(behind[places], jnp.concatenate([high, high, low], axis=0))

    for copy in table_copies:
        copy.wait()

    @pl.loop(0, CHANNELS // TILE)
    def _(tile):
        cols = columns(tile)
        block = taps[cols]
        table = ahead[:, pl.ds(EARLY_HALO, 2 * TAPS)]
        spec = matmul_nt(table, jnp.concatenate([block, block], axis=1))
        tap_spec[pl.ds(0, HALF), cols] = spec[:HALF] + skip[:, cols]
        tap_spec[pl.ds(HALF, HALF), cols] = spec[HALF:]
        mixed_spec[:, cols] = spectrum(LATE_BLOCK, mixed[:, cols])

    def block_rows(kind, core):
        low = y[0] if kind in ("here", "above") else 1 - y[0]
        return weight_rows(low, odd if kind in ("here", "beside") else 1 - odd, core)

    kinds = ("here", "beside", "above", "corner")
    others = pl.ds((1 - dp) * 2, 2)
    from_core = {kind: gather(full_weight.at[others, block_rows(kind, 1 - core)]) for kind in kinds}
    from_side = gather(full_weight.at[others, block_rows("above", core)])
    from_corner = [
        gather(full_weight.at[(1 - dp) * 2 + i, block_rows("corner", core)]) for i in range(2)
    ]
    near_copies = []

    def weight_spot(kind, number):
        part = pl.ds(pl.multiple_of(block_rows(kind, core).start + number % 4 * 32, 32), 32)
        return full_weight.at[(1 - dp) * 2 + number // 4, part]

    def share_core(kind, i):
        spot = full_weight.at[(1 - dp) * 2 + i, block_rows(kind, core)]
        send(spot, spot, to_core, from_core[kind])

    def share_import(number):
        imports[number].wait_recv()
        spot = weight_spot("here", number)
        near_copies.append(send(spot, spot, to_near))
        send(spot, spot, to_side[number % 2], from_side)
        if number % 4 == 3:
            share_core("here", number // 4)

    def share_near(number):
        near_copies[number].wait_recv()
        spot = weight_spot("beside", number)
        send(spot, spot, to_side[number % 2], from_corner[number // 4])
        if number % 4 == 3:
            share_core("beside", number // 4)

    def convolve(start):
        @pl.loop(start, start + 2)
        def _(tile):
            cols = columns(tile)
            halo = jnp.where(seq > 0, mixed_halo[:, cols], jnp.zeros((TAPS, TILE), BF16))
            spec = mixed_spec[:, cols] + spectrum(EARLY_HALO, halo)
            mixed_spec[:, cols] = spec
            real, imag = spec[:HALF], spec[HALF:]
            tap_real, tap_imag = tap_spec[pl.ds(0, HALF), cols], tap_spec[pl.ds(HALF, HALF), cols]
            value_now = restore(
                pl.ds(0, ROWS),
                real * tap_real - imag * tap_imag,
                real * tap_imag + imag * tap_real,
            )
            state[:, cols] = value_now
            gated[pl.ds(0, ROWS), cols] = (query[:, cols].astype(F32) * value_now).astype(BF16)

    for copy in state_copies:
        copy.wait()
    mixed_sent.wait_recv()

    share_import(0)
    convolve(0)
    share_import(1)
    convolve(2)
    gated_sent = send(gated.at[pl.ds(0, ROWS)], gated.at[pl.ds(ROWS, ROWS)], to_core)

    first = [
        [gather(landing[quarter * PER_QUARTER + stream]) for stream in range(STREAMS)]
        for quarter in range(4)
    ]

    def lanes_of(stream):
        return pl.ds(stream * LANES, LANES)

    def first_view(quarter, slot, stream):
        if quarter < 2:
            return partial.at[quarter, slot[0], slot[1], slot[2], :, lanes_of(stream)]
        return partial.at[quarter, slot[0], slot[1], :, :, lanes_of(stream)]

    def first_landing(quarter, chunk, i, stream):
        landed = landing[quarter * PER_QUARTER + stream]
        return landed.at[chunk] if quarter < 2 else landed.at[chunk, i]

    first_targets = [to_near, to_far, to_side[0], to_side[1]]

    def products(chunk, owner):
        low, group = lax.div(owner, 2), pl.ds(lax.rem(owner, 2) * 4, 4)

        @pl.loop(0, 4)
        def _(quarter):
            rows = turned[pl.ds(owner * 4, 4)].reshape(512, 2 * ROWS)
            block = matmul(rows, gated[:, columns(quarter)]).astype(BF16)
            partial[quarter, low, group] = block.reshape(4, 2, 64, TILE)

    def halve(chunk, owner, stream):
        for quarter in range(4):
            for i, slot in enumerate(first_slots(quarter, owner, y, z, False)):
                send(
                    first_view(quarter, slot, stream),
                    first_landing(quarter, chunk, i, stream),
                    first_targets[quarter],
                    first[quarter][stream],
                )

    share_import(2)
    right_top.wait_recv()
    forward_right = pass_cot(left, top, to_right)
    left_bottom.wait_recv()
    forward_left = pass_cot(right, bottom, to_left)
    turned_left = [turn(left, 0, 128)]
    turned_right = [turn(right, 128, 128)]
    share_import(3)
    share_near(0)
    turned_own.wait_recv()
    gated_sent.wait_recv()
    products(0, tp)
    halve(0, tp, 0)
    share_import(4)
    share_near(1)
    share_import(5)
    share_near(2)
    share_import(6)
    share_near(3)
    right_bottom.wait_recv()
    turned_left.append(turn(left, 128, 128))
    left_top.wait_recv()
    turned_right.append(turn(right, 0, 128))
    for copy in own:
        copy.wait()
    late = jnp.where(lax.div(across, 2) == dp, across, dp * 4 + 1 - tp)
    early = dp * 4 + 1 - late

    @pl.loop(0, CHANNELS // TILE)
    def _(tile):
        cols = columns(tile)
        grad_gated[:, cols] = matmul_nt(full_cot[early], full_weight[early, cols])

    share_import(7)
    share_near(4)
    for copy in turned_left:
        copy.wait_recv()
    products(1, left)
    halve(1, left, 0)
    share_near(5)
    share_near(6)
    for copy in turned_right:
        copy.wait_recv()
    products(2, right)
    halve(2, right, 0)
    forward_right.wait_recv()
    forward_left.wait_recv()
    turned_across = turn(across, 0, ROWS)
    share_near(7)
    halve(0, tp, 1)
    halve(1, left, 1)
    @pl.loop(0, CHANNELS // TILE)
    def _(tile):
        cols = columns(tile)
        grad_gated[:, cols] += matmul_nt(full_cot[late], full_weight[late, cols])

    turned_across.wait_recv()
    products(3, across)
    halve(3, across, 0)
    halve(2, right, 1)
    halve(3, across, 1)

    from_side[0].wait_recv()
    share_core("above", 0)
    share_core("above", 1)
    from_corner[0][0].wait_recv()
    share_core("corner", 0)
    signal_sent = gather(signal_halo)

    def finish(tile, kind):
        from_core[kind][0].wait_recv()
        cols = columns(tile)
        total = grad_gated[:, cols]
        for i in range(2):
            owner = (1 - dp) * 2 + i
            total = total + matmul_nt(full_cot[owner], full_weight[owner, cols])
        made_query[:, cols] = (total * state[:, cols]).astype(BF16)
        signal[:, cols] = (total * query[:, cols].astype(F32)).astype(BF16)
        send(signal.at[top, cols], signal_halo.at[:, cols], to_prior, signal_sent)
        spec = spectrum(EARLY_BLOCK, signal[:, cols])
        signal_spec[:, cols] = spec
        real, imag = spec[:HALF], spec[HALF:]
        part_real, part_imag = mixed_spec[pl.ds(0, HALF), cols], mixed_spec[pl.ds(HALF, HALF), cols]
        lags = restore(
            pl.ds(2 * ROWS, TAPS),
            real * part_real + imag * part_imag,
            imag * part_real - real * part_imag,
        )
        for i in range(TILE // 128):
            block = lags[:, i * 128 : (i + 1) * 128].T
            lag_sum[tile * (TILE // 128) + i] = block.astype(BF16)

    rounds = {}

    def exchange(quarter, step, stream):
        axis, move = PLANS[quarter][step]
        there_y = move(y) if axis == "y" else y
        there_z = move(z) if axis == "z" else z
        landed = landing[quarter * PER_QUARTER + step * STREAMS + stream]
        group = gather(landed)
        for i, slot in enumerate(slots(PLANS[quarter], step, there_y, there_z)):
            view = slot_view(partial, quarter, slot, lanes_of(stream))
            send(view, landed.at[i], place(there_y, there_z, core), group)
        rounds[quarter, step, stream] = group[0], landed

    def combine(quarter, step, stream):
        lanes = lanes_of(stream)
        if step == 0:
            first[quarter][stream][0].wait_recv()
            pairs = [
                (first_view(quarter, slot, stream), first_landing(quarter, chunk, i, stream))
                for chunk, owner in enumerate((tp, left, right, across))
                for i, slot in enumerate(first_slots(quarter, owner, y, z, True))
            ]
        else:
            copy, landed = rounds[quarter, step, stream]
            copy.wait_recv()
            pairs = [
                (slot_view(partial, quarter, slot, lanes), landed.at[i])
                for i, slot in enumerate(slots(PLANS[quarter], step, y, z))
            ]
        for view, landed in pairs:
            total = view[...].astype(F32) + landed[...].astype(F32)
            if step < 4:
                view[...] = total.astype(BF16)
            else:
                place_out = pl.ds(quarter * TILE + stream * LANES, LANES)
                made_weight[:, place_out] = total * scale
        if step < 4:
            exchange(quarter, step + 1, stream)

    def combine_all(step, stream):
        for quarter in range(4):
            combine(quarter, step, stream)

    def restore_back(start):
        @pl.loop(start, start + 2)
        def _(tile):
            cols = columns(tile)
            halo = jnp.where(seq < 31, signal_halo[:, cols], jnp.zeros((TAPS, TILE), BF16))
            spec = signal_spec[:, cols] + spectrum(LATE_HALO, halo)
            real, imag = spec[:HALF], spec[HALF:]
            tap_real, tap_imag = tap_spec[pl.ds(0, HALF), cols], tap_spec[pl.ds(HALF, HALF), cols]
            back = restore(
                pl.ds(ROWS, ROWS),
                real * tap_real + imag * tap_imag,
                imag * tap_real - real * tap_imag,
            )
            made_key[:, cols] = (back * value[:, cols].astype(F32)).astype(BF16)
            made_value[:, cols] = (back * key[:, cols].astype(F32)).astype(BF16)

    finish(y[0] * 2 + odd, "here")
    finish((1 - y[0]) * 2 + odd, "beside")
    from_corner[1][0].wait_recv()
    share_core("corner", 1)
    finish(y[0] * 2 + 1 - odd, "above")
    finish((1 - y[0]) * 2 + 1 - odd, "corner")

    near_sums = gather(near_land)
    for i in range(1, 8):
        send(lag_sum.at[members[i]], near_land.at[i - 1], to_member(members[i]), near_sums, 0)

    combine_all(0, 0)
    combine_all(0, 1)
    near_sums[0].wait_recv()
    total = lag_sum[member].astype(F32)
    for i in range(7):
        total = total + near_land[i].astype(F32)
    lag_mid[...] = total.reshape(8, 16, TAPS)
    far_sums = gather(far_land)
    for i in range(1, 8):
        send(lag_mid.at[heights[i]], far_land.at[i - 1], place(y, heights[i], core), far_sums, 1)

    combine_all(1, 0)
    signal_sent[0].wait_recv()

    restore_back(0)
    combine_all(1, 1)
    combine_all(2, 0)
    far_sums[0].wait_recv()
    total = lag_mid[z]
    for i in range(7):
        total = total + far_land[i]
    lag_out[member, z] = (total * scale).astype(BF16)
    mine = lag_out.at[member, z]
    copies = [send(mine, mine, place(y, heights[i], core), None, 2) for i in range(1, 8)]
    restore_back(2)
    combine_all(2, 1)
    combine_all(3, 0)
    for copy in copies:
        copy.wait_recv()
    mine = lag_out.at[member]
    copies = [send(mine, mine, to_member(members[i]), None, 3) for i in range(1, 8)]
    combine_all(3, 1)
    combine_all(4, 0)
    for copy in copies:
        copy.wait_recv()
    made_filter[...] = lag_out[...].astype(F32)
    diagonal = lax.broadcasted_iota(jnp.int32, (128, 128), 0) == lax.broadcasted_iota(
        jnp.int32, (128, 128), 1
    )
    for i in range(8):
        first_lag = made_filter[i].reshape(128, TAPS)[:, 0:1]
        spread = jnp.where(diagonal, jnp.broadcast_to(first_lag, (128, 128)), 0.0)
        made_skip[pl.ds(i, 1)] = jnp.sum(spread, axis=0, keepdims=True)
    combine_all(4, 1)
    sent = [near_land, far_land, near_land.at[:, pl.ds(0, 16)], near_land]
    for size in started:
        planes = planes_of(size)
        sent.append(full_weight.at[pl.ds(0, planes), pl.ds(0, size // 2048 // planes)])
    for out_number, block in enumerate(sent):
        describe(block, block, to_core, 0, out_number).wait_send()


def hand_on(*refs):
    count = (len(refs) - 1) // 2
    copies = [
        pltpu.make_async_copy(refs[i], refs[count + i], refs[-1].at[i]) for i in range(count)
    ]
    for copy in copies:
        copy.start()
    for copy in copies:
        copy.wait()


def per_device(query_gate, key_gate, value_input, filter_taps, skip_gain, out_weight, cotangent):
    ahead, behind = spectrum_tables()
    anywhere = pl.BlockSpec(memory_space=pl.ANY)
    block = ((ROWS, CHANNELS), BF16)
    scratch = [
        block,
        block,
        block,
        ((CHANNELS, TAPS), BF16),
        ((1, CHANNELS), F32),
        (ahead.shape, BF16),
        (behind.shape, BF16),
        ((4, ROWS, 1024), BF16),
        ((4, CHANNELS, 1024), BF16),
        ((16, 128, 2 * ROWS), BF16),
        ((16, 128, ROWS), BF16),
        ((2 * ROWS, CHANNELS), BF16),
        block,
        ((TAPS, CHANNELS), BF16),
        block,
        ((TAPS, CHANNELS), BF16),
        ((SIZE, CHANNELS), F32),
        ((SIZE, CHANNELS), F32),
        ((SIZE, CHANNELS), F32),
        ((ROWS, CHANNELS), F32),
        ((ROWS, CHANNELS), F32),
        ((4, 2, 8, 2, 64, TILE), BF16),
        ((8, 128, TAPS), BF16),
        ((8, 8, 16, TAPS), BF16),
        ((7, 128, TAPS), BF16),
        ((8, 16, TAPS), F32),
        ((7, 16, TAPS), F32),
    ]
    results = pl.pallas_call(
        kernel,
        out_shape=[
            pltpu.VMEM((ROWS, CHANNELS), BF16),
            pltpu.VMEM((ROWS, CHANNELS), BF16),
            pltpu.VMEM((ROWS, CHANNELS), BF16),
            pltpu.VMEM((8, 8, 16, TAPS), F32),
            pltpu.VMEM((8, 128), F32),
            pltpu.VMEM((64, CHANNELS), F32),
        ],
        in_specs=[anywhere] * 9,
        out_specs=[pl.BlockSpec(memory_space=pltpu.VMEM)] * 6,
        scratch_shapes=[pltpu.VMEM(shape, dtype) for shape, dtype in scratch]
        + [
            pltpu.SemaphoreType.DMA((OUT_EXTRA + OUT_SETS,)),
            pltpu.SemaphoreType.DMA((COPIES,)),
            pltpu.SemaphoreType.DMA((10,)),
        ]
        + [pltpu.VMEM(shape, BF16) for shape in landing_shapes()],
        compiler_params=pltpu.CompilerParams(
            collective_id=0, has_side_effects=True, vmem_limit_bytes=56 * 1024 * 1024
        ),
    )(
        query_gate[0], key_gate[0], value_input[0], filter_taps, skip_gain[None, :],
        out_weight, cotangent[0], jnp.asarray(ahead), jnp.asarray(behind),
    )
    results = [
        results[0][None],
        results[1][None],
        results[2][None],
        results[3].reshape(CHANNELS, TAPS),
        results[4].reshape(CHANNELS),
        results[5],
    ]
    return tuple(
        pl.pallas_call(
            hand_on,
            out_shape=[jax.ShapeDtypeStruct(x.shape, x.dtype) for x in results],
            in_specs=[pl.BlockSpec(memory_space=pltpu.VMEM)] * 6,
            out_specs=[anywhere] * 6,
            scratch_shapes=[pltpu.SemaphoreType.DMA((6,))],
        )(*[pltpu.with_memory_space_constraint(x, pltpu.VMEM) for x in results])
    )


def solution(mesh):
    return jax.shard_map(
        per_device,
        mesh=mesh,
        in_specs=(
            P("dp", "seq", "tp"),
            P("dp", "seq", "tp"),
            P("dp", "seq", "tp"),
            P("tp", None),
            P("tp"),
            P("tp", "dp"),
            P("dp", "seq", "tp"),
        ),
        out_specs=(
            P("dp", "seq", "tp"),
            P("dp", "seq", "tp"),
            P("dp", "seq", "tp"),
            P("tp", None),
            P("tp"),
            P(("seq", "dp"), "tp"),
        ),
        check_vma=False,
    )
```

```python
import itertools
import math

import jax
import jax.numpy as jnp
import ml_dtypes
import numpy as np
from jax import lax
from jax.experimental import pallas as pl
from jax.experimental.pallas import tpu as pltpu
from jax.sharding import PartitionSpec as P

ROWS = 256
TAPS = 128
SIZE = ROWS + TAPS
HALF = SIZE // 2
CHANNELS = 1024
TILE = 256
STREAMS = 2
LANES = TILE // STREAMS
PER_QUARTER = 5 * STREAMS
SENT_ROWS = 2048
OUT_EXTRA, OUT_SETS = 4, 3
COPIES = 96
BF16 = jnp.bfloat16
F32 = jnp.float32


PARTS = ((TAPS, ROWS), (0, TAPS), (0, ROWS), (ROWS, TAPS))
LATE_BLOCK, EARLY_HALO, EARLY_BLOCK, LATE_HALO = 0, 2 * ROWS, 2 * SIZE, 2 * SIZE + 2 * ROWS


def split_table(table):
    high = table.astype(ml_dtypes.bfloat16)
    return high, (table - high.astype(np.float64)).astype(ml_dtypes.bfloat16)


def spectrum_tables():
    odd = 2 * np.arange(HALF) + 1

    def angles(positions):
        return np.pi * ((odd[:, None] * positions[None, :]) % (2 * SIZE)) / SIZE

    ahead = angles(np.arange(SIZE))
    forward = np.concatenate([np.cos(ahead), -np.sin(ahead)], axis=0)
    places = np.concatenate(
        [np.arange(TAPS, SIZE), np.arange(ROWS), np.arange(-TAPS, 0)]
    )
    behind = angles(places).T
    inverse = (2.0 / SIZE) * np.concatenate([np.cos(behind), -np.sin(behind)], axis=1)
    high, low = split_table(forward)
    pieces = [piece[:, start : start + size] for start, size in PARTS for piece in (high, low)]
    back_high, back_low = split_table(inverse)
    return (
        np.concatenate(pieces, axis=1),
        np.concatenate([back_high, back_low, back_high], axis=1),
    )


def matmul(left, right):
    return jnp.dot(left, right, preferred_element_type=F32)


def matmul_nt(left, right):
    return lax.dot_general(
        left, right, (((1,), (1,)), ((), ())), preferred_element_type=F32
    )


def y_near(y):
    return (1 - y[0], y[1])


def y_far(y):
    return (1 - y[0], 1 - y[1])


def z_up(z):
    return z + 1 - 2 * lax.rem(z, 2)


def z_down(z):
    return lax.rem(z + 2 * lax.rem(z, 2) + 7, 8)


def z_three(z):
    return lax.rem(z + 11 - 6 * lax.rem(z, 2), 8)


def z_back_three(z):
    return lax.rem(z + 5 + 6 * lax.rem(z, 2), 8)


PLANS = (
    (("y", y_near), ("y", y_far), ("z", z_up), ("z", z_down), ("z", z_three)),
    (("y", y_far), ("y", y_near), ("z", z_down), ("z", z_up), ("z", z_back_three)),
    (("z", z_up), ("z", z_down), ("y", y_near), ("y", y_far), ("z", z_three)),
    (("z", z_down), ("z", z_up), ("y", y_far), ("y", y_near), ("z", z_back_three)),
)


def kept(rest, place):
    if not rest:
        return [place]
    return kept(rest[1:], place) + kept(rest[1:], rest[0](place))


def remaining(plan, step, axis):
    return [move for name, move in plan[step + 1 :] if name == axis]


def slots(plan, step, y, z):
    y_rest, z_rest = remaining(plan, step, "y"), remaining(plan, step, "z")
    y_list = [None] if len(y_rest) == 2 else kept(y_rest, y)
    z_list = [None] if len(z_rest) == 3 else kept(z_rest, z)
    return [(one, other) for one in y_list for other in z_list]


def slot_view(ref, quarter, slot, lanes):
    y, z = slot
    if y is None:
        return ref.at[quarter, :, z, :, :, lanes]
    if z is None:
        return ref.at[quarter, y[0], :, y[1], :, lanes]
    return ref.at[quarter, y[0], z, y[1], :, lanes]


def planes_of(size):
    for planes in range(1, 5):
        if size % (2048 * 16 * planes) == 0 and size // (2048 * planes) <= 1024:
            return planes
    return None


def landing_shapes():
    shapes = []
    for plan in PLANS:
        shapes += [(4, 4, 64, LANES) if plan[0][0] == "y" else (4, 2, 2, 64, LANES)] * STREAMS
        for step in range(1, 5):
            y_rest, z_rest = remaining(plan, step, "y"), remaining(plan, step, "z")
            if len(y_rest) == 2:
                shape = (2 ** len(z_rest), 2, 2, 64, LANES)
            elif len(z_rest) == 3:
                shape = (2 ** len(y_rest), 8, 64, LANES)
            else:
                shape = (2 ** (len(y_rest) + len(z_rest)), 64, LANES)
            shapes += [shape] * STREAMS
    return shapes


def first_slots(quarter, owner, y, z, keep):
    low, half = lax.div(owner, 2), lax.rem(owner, 2)
    group = pl.ds(half * 4, 4)
    other = 0 if keep else 1
    if quarter == 0:
        return [(low, group, lax.rem(y[1] + y[0] + low + other, 2))]
    if quarter == 1:
        return [(low, group, lax.rem(y[1] + other, 2))]
    if quarter == 2:
        kind = lax.rem(lax.div(lax.rem(z, 4) + 1, 2) + other, 2)
        return [(low, half * 4 + kind + i * (3 - 2 * kind)) for i in range(2)]
    kind = lax.rem(lax.div(lax.rem(z, 4), 2) + other, 2)
    return [(low, half * 4 + kind * 2 + i) for i in range(2)]


def kernel(
    query_in, key_in, value_in, taps_in, skip_in, weight, cot, ahead_in, behind_in,
    made_query, made_key, made_value, made_filter, made_skip, made_weight,
    query, key, value, taps, skip, ahead, behind,
    full_cot, full_weight, turned, turned_away, gated, mixed, mixed_halo, signal, signal_halo,
    tap_spec, mixed_spec, signal_spec, state, grad_gated, partial, lag_sum, lag_out,
    near_land, lag_mid, far_land, send_sem, recv_sem, local_sem, *landing,
):
    seq, tp, dp = lax.axis_index("seq"), lax.axis_index("tp"), lax.axis_index("dp")
    core = lax.rem(seq, 2)
    z = lax.rem(lax.div(seq, 2), 8)
    y = (lax.div(seq, 16), dp)
    scale = 1.0 / math.sqrt(2 * 32 * ROWS)

    def place(y, z, core):
        return ((y[0] * 8 + z) * 2 + core, tp, y[1])

    right, left, across = lax.rem(tp + 1, 4), lax.rem(tp + 3, 4), lax.rem(tp + 2, 4)
    to_right, to_left = (seq, right, dp), (seq, left, dp)
    to_next, to_prior = (lax.rem(seq + 1, 32), tp, dp), (lax.rem(seq + 31, 32), tp, dp)
    to_core = place(y, z, 1 - core)
    to_near, to_far = place(y_near(y), z, core), place(y_far(y), z, core)
    to_side = [place(y, z_up(z), core), place(y, z_down(z), core)]
    member = (y[1] * 2 + y[0]) * 2 + core

    def to_member(index):
        high = lax.div(index, 4)
        return place((lax.rem(lax.div(index, 2), 2), high), z, lax.rem(index, 2))

    members = [lax.rem(member + i, 8) for i in range(8)]
    heights = [lax.rem(z + i, 8) for i in range(8)]

    barrier = pltpu.get_barrier_semaphore()
    greeted = [to_right, to_left, to_next, to_prior]
    greeted += [to_member(members[i]) for i in range(1, 8)]
    greeted += [place(y, heights[i], core) for i in range(1, 8)]
    for target in greeted:
        pl.semaphore_signal(
            barrier, inc=1, device_id=target, device_id_type=pl.DeviceIdType.MESH
        )

    local_numbers = itertools.count()

    def fetch(source, target):
        copy = pltpu.make_async_copy(source, target, local_sem.at[next(local_numbers)])
        copy.start()
        return copy

    key_copy, value_copy = fetch(key_in, key), fetch(value_in, value)
    cot_copy = fetch(cot, full_cot.at[tp])
    table_copies = [fetch(ahead_in, ahead), fetch(taps_in, taps), fetch(skip_in, skip)]
    state_copies = [fetch(behind_in, behind), fetch(query_in, query)]
    key_copy.wait()
    value_copy.wait()
    mixed[...] = (key[...].astype(F32) * value[...].astype(F32)).astype(BF16)
    pl.semaphore_wait(barrier, len(greeted))

    numbers = itertools.count()
    started = []

    def describe(source, target_ref, target, number, out_number):
        return pltpu.make_async_remote_copy(
            src_ref=source,
            dst_ref=target_ref,
            send_sem=send_sem.at[out_number],
            recv_sem=recv_sem.at[number],
            device_id=target,
            device_id_type=pl.DeviceIdType.MESH,
        )

    def send(source, target_ref, target, group=None, out=None):
        size = math.prod(source.shape) * source.dtype.itemsize
        if out is None:
            if not started or started[-1] >= SENT_ROWS * 2048 and planes_of(started[-1]):
                started.append(0)
            started[-1] += size
        number = next(numbers) if group is None else group[1]
        out_number = OUT_EXTRA + len(started) - 1 if out is None else out
        copy = describe(source, target_ref, target, number, out_number)
        copy.start()
        return copy

    def gather(landed):
        number = next(numbers)
        return describe(landed, landed, to_core, number, 0), number

    top, bottom = pl.ds(0, 128), pl.ds(128, 128)

    def pass_cot(owner, part, target):
        spot = full_cot.at[owner, part]
        return send(spot, spot, target)

    right_top = send(cot.at[top], full_cot.at[tp, top], to_right)
    left_bottom = send(cot.at[bottom], full_cot.at[tp, bottom], to_left)

    def weight_rows(low, odd, core):
        return pl.ds(pl.multiple_of(((low * 2 + odd) * 2 + core) * 128, 128), 128)

    odd = lax.rem(z, 2)
    given = weight_rows(1 - y[0], odd, core)
    imports = []
    for i in range(2):
        for r in range(4):
            rows = pl.ds(pl.multiple_of(given.start + r * 32, 32), 32)
            source = weight.at[rows, pl.ds(i * 1024, 1024)]
            imports.append(send(source, full_weight.at[dp * 2 + i, rows], to_far))
    right_bottom = send(cot.at[bottom], full_cot.at[tp, bottom], to_right)
    left_top = send(cot.at[top], full_cot.at[tp, top], to_left)
    own = [fetch(weight.at[:, pl.ds(i * 1024, 1024)], full_weight.at[dp * 2 + i]) for i in range(2)]

    wide = [pl.ds(h * 2 * TILE, 2 * TILE) for h in range(2)]
    mixed_sent = [send(mixed.at[bottom, cols], mixed_halo.at[:, cols], to_next) for cols in wide]

    def turn(owner, start, size):
        tokens, far_tokens = pl.ds(start, size), pl.ds(ROWS + start, size)
        for i in range(4):
            mine = pl.ds(pl.multiple_of((i * 2 + core) * 128, 128), 128)
            other = pl.ds(pl.multiple_of((i * 2 + 1 - core) * 128, 128), 128)
            turned[owner * 4 + i, :, tokens] = full_cot[owner, tokens, mine].T
            turned_away[owner * 4 + i, :, tokens] = full_cot[owner, tokens, other].T
        group = pl.ds(owner * 4, 4)
        return send(turned_away.at[group, :, tokens], turned.at[group, :, far_tokens], to_core)

    cot_copy.wait()
    turned_own = turn(tp, 0, ROWS)

    def columns(tile):
        return pl.ds(pl.multiple_of(tile * TILE, TILE), TILE)

    def spectrum(start, block):
        table = ahead[:, pl.ds(start, 2 * block.shape[0])]
        return matmul(table, jnp.concatenate([block, block], axis=0))

    def restore(places, real, imag):
        spec = jnp.concatenate([real, imag], axis=0)
        high = spec.astype(BF16)
        low = (spec - high.astype(F32)).astype(BF16)
        return matmul(behind[places], jnp.concatenate([high, high, low], axis=0))

    for copy in table_copies:
        copy.wait()

    @pl.loop(0, CHANNELS // TILE)
    def _(tile):
        cols = columns(tile)
        block = taps[cols]
        table = ahead[:, pl.ds(EARLY_HALO, 2 * TAPS)]
        spec = matmul_nt(table, jnp.concatenate([block, block], axis=1))
        tap_spec[pl.ds(0, HALF), cols] = spec[:HALF] + skip[:, cols]
        tap_spec[pl.ds(HALF, HALF), cols] = spec[HALF:]
        mixed_spec[:, cols] = spectrum(LATE_BLOCK, mixed[:, cols])

    def block_rows(kind, core):
        low = y[0] if kind in ("here", "above") else 1 - y[0]
        return weight_rows(low, odd if kind in ("here", "beside") else 1 - odd, core)

    kinds = ("here", "beside", "above", "corner")
    others = pl.ds((1 - dp) * 2, 2)
    from_core = {kind: gather(full_weight.at[others, block_rows(kind, 1 - core)]) for kind in kinds}
    from_side = gather(full_weight.at[others, block_rows("above", core)])
    from_corner = [
        gather(full_weight.at[(1 - dp) * 2 + i, block_rows("corner", core)]) for i in range(2)
    ]
    near_copies = []

    def weight_spot(kind, number):
        part = pl.ds(pl.multiple_of(block_rows(kind, core).start + number % 4 * 32, 32), 32)
        return full_weight.at[(1 - dp) * 2 + number // 4, part]

    def share_core(kind, i):
        spot = full_weight.at[(1 - dp) * 2 + i, block_rows(kind, core)]
        send(spot, spot, to_core, from_core[kind])

    def share_import(number):
        imports[number].wait_recv()
        spot = weight_spot("here", number)
        near_copies.append(send(spot, spot, to_near))
        send(spot, spot, to_side[number % 2], from_side)
        if number % 4 == 3:
            share_core("here", number // 4)

    def share_near(number):
        near_copies[number].wait_recv()
        spot = weight_spot("beside", number)
        send(spot, spot, to_side[number % 2], from_corner[number // 4])
        if number % 4 == 3:
            share_core("beside", number // 4)

    def convolve(start):
        @pl.loop(start, start + 2)
        def _(tile):
            cols = columns(tile)
            halo = jnp.where(seq > 0, mixed_halo[:, cols], jnp.zeros((TAPS, TILE), BF16))
            spec = mixed_spec[:, cols] + spectrum(EARLY_HALO, halo)
            mixed_spec[:, cols] = spec
            real, imag = spec[:HALF], spec[HALF:]
            tap_real, tap_imag = tap_spec[pl.ds(0, HALF), cols], tap_spec[pl.ds(HALF, HALF), cols]
            value_now = restore(
                pl.ds(0, ROWS),
                real * tap_real - imag * tap_imag,
                real * tap_imag + imag * tap_real,
            )
            state[:, cols] = value_now
            gated[pl.ds(0, ROWS), cols] = (query[:, cols].astype(F32) * value_now).astype(BF16)

    for copy in state_copies:
        copy.wait()
    gated_sent = []
    for h in range(2):
        mixed_sent[h].wait_recv()
        convolve(2 * h)
        half = gated.at[pl.ds(0, ROWS), wide[h]]
        gated_sent.append(send(half, gated.at[pl.ds(ROWS, ROWS), wide[h]], to_core))

    first = [
        [gather(landing[quarter * PER_QUARTER + stream]) for stream in range(STREAMS)]
        for quarter in range(4)
    ]

    def lanes_of(stream):
        return pl.ds(stream * LANES, LANES)

    def first_view(quarter, slot, stream):
        if quarter < 2:
            return partial.at[quarter, slot[0], slot[1], slot[2], :, lanes_of(stream)]
        return partial.at[quarter, slot[0], slot[1], :, :, lanes_of(stream)]

    def first_landing(quarter, chunk, i, stream):
        landed = landing[quarter * PER_QUARTER + stream]
        return landed.at[chunk] if quarter < 2 else landed.at[chunk, i]

    first_targets = [to_near, to_far, to_side[0], to_side[1]]

    def products(owner, start=0, stop=4):
        low, group = lax.div(owner, 2), pl.ds(lax.rem(owner, 2) * 4, 4)

        @pl.loop(start, stop)
        def _(quarter):
            rows = turned[pl.ds(owner * 4, 4)].reshape(512, 2 * ROWS)
            block = matmul(rows, gated[:, columns(quarter)]).astype(BF16)
            partial[quarter, low, group] = block.reshape(4, 2, 64, TILE)

    def halve(chunk, owner, stream, quarters=(0, 1, 2, 3)):
        for quarter in quarters:
            for i, slot in enumerate(first_slots(quarter, owner, y, z, False)):
                send(
                    first_view(quarter, slot, stream),
                    first_landing(quarter, chunk, i, stream),
                    first_targets[quarter],
                    first[quarter][stream],
                )

    share_import(0)
    share_import(1)
    turned_own.wait_recv()
    gated_sent[0].wait_recv()
    products(tp, 0, 2)
    halve(0, tp, 0, (0, 1))
    halve(0, tp, 1, (1,))
    share_import(2)
    gated_sent[1].wait_recv()
    products(tp, 2, 4)
    for stream in range(STREAMS):
        halve(0, tp, stream, (2, 3))
    right_top.wait_recv()
    forward_right = pass_cot(left, top, to_right)
    left_bottom.wait_recv()
    forward_left = pass_cot(right, bottom, to_left)
    share_import(3)
    share_near(0)
    turned_left = [turn(left, 0, 128)]
    turned_right = [turn(right, 128, 128)]
    share_import(4)
    share_import(5)
    share_import(6)
    right_bottom.wait_recv()
    turned_left.append(turn(left, 128, 128))
    left_top.wait_recv()
    turned_right.append(turn(right, 0, 128))
    share_import(7)
    share_near(1)
    share_near(2)
    for copy in own:
        copy.wait()
    late = jnp.where(lax.div(across, 2) == dp, across, dp * 4 + 1 - tp)
    early = dp * 4 + 1 - late

    @pl.loop(0, CHANNELS // TILE)
    def _(tile):
        cols = columns(tile)
        grad_gated[:, cols] = matmul_nt(full_cot[early], full_weight[early, cols])

    share_near(3)
    for copy in turned_left:
        copy.wait_recv()
    products(left)
    halve(1, left, 0)
    share_near(4)
    share_near(5)
    for copy in turned_right:
        copy.wait_recv()
    products(right)
    halve(2, right, 0)
    forward_right.wait_recv()
    forward_left.wait_recv()
    turned_across = turn(across, 0, ROWS)
    share_near(6)
    share_near(7)
    halve(0, tp, 1, (0,))
    halve(1, left, 1)
    @pl.loop(0, CHANNELS // TILE)
    def _(tile):
        cols = columns(tile)
        grad_gated[:, cols] += matmul_nt(full_cot[late], full_weight[late, cols])

    turned_across.wait_recv()
    products(across)
    halve(3, across, 0)
    halve(2, right, 1)
    halve(3, across, 1)

    from_side[0].wait_recv()
    share_core("above", 0)
    share_core("above", 1)
    from_corner[0][0].wait_recv()
    share_core("corner", 0)
    signal_sent = gather(signal_halo)

    def finish(tile, kind):
        from_core[kind][0].wait_recv()
        cols = columns(tile)
        total = grad_gated[:, cols]
        for i in range(2):
            owner = (1 - dp) * 2 + i
            total = total + matmul_nt(full_cot[owner], full_weight[owner, cols])
        made_query[:, cols] = (total * state[:, cols]).astype(BF16)
        signal[:, cols] = (total * query[:, cols].astype(F32)).astype(BF16)
        send(signal.at[top, cols], signal_halo.at[:, cols], to_prior, signal_sent)
        spec = spectrum(EARLY_BLOCK, signal[:, cols])
        signal_spec[:, cols] = spec
        real, imag = spec[:HALF], spec[HALF:]
        part_real, part_imag = mixed_spec[pl.ds(0, HALF), cols], mixed_spec[pl.ds(HALF, HALF), cols]
        lags = restore(
            pl.ds(2 * ROWS, TAPS),
            real * part_real + imag * part_imag,
            imag * part_real - real * part_imag,
        )
        for i in range(TILE // 128):
            block = lags[:, i * 128 : (i + 1) * 128].T
            lag_sum[tile * (TILE // 128) + i] = block.astype(BF16)

    rounds = {}

    def exchange(quarter, step, stream):
        axis, move = PLANS[quarter][step]
        there_y = move(y) if axis == "y" else y
        there_z = move(z) if axis == "z" else z
        landed = landing[quarter * PER_QUARTER + step * STREAMS + stream]
        group = gather(landed)
        for i, slot in enumerate(slots(PLANS[quarter], step, there_y, there_z)):
            view = slot_view(partial, quarter, slot, lanes_of(stream))
            send(view, landed.at[i], place(there_y, there_z, core), group)
        rounds[quarter, step, stream] = group[0], landed

    def combine(quarter, step, stream):
        lanes = lanes_of(stream)
        if step == 0:
            first[quarter][stream][0].wait_recv()
            pairs = [
                (first_view(quarter, slot, stream), first_landing(quarter, chunk, i, stream))
                for chunk, owner in enumerate((tp, left, right, across))
                for i, slot in enumerate(first_slots(quarter, owner, y, z, True))
            ]
        else:
            copy, landed = rounds[quarter, step, stream]
            copy.wait_recv()
            pairs = [
                (slot_view(partial, quarter, slot, lanes), landed.at[i])
                for i, slot in enumerate(slots(PLANS[quarter], step, y, z))
            ]
        for view, landed in pairs:
            total = view[...].astype(F32) + landed[...].astype(F32)
            if step < 4:
                view[...] = total.astype(BF16)
            else:
                place_out = pl.ds(quarter * TILE + stream * LANES, LANES)
                made_weight[:, place_out] = total * scale
        if step < 4:
            exchange(quarter, step + 1, stream)

    def combine_all(step, stream):
        for quarter in range(4):
            combine(quarter, step, stream)

    def restore_back(start):
        @pl.loop(start, start + 2)
        def _(tile):
            cols = columns(tile)
            halo = jnp.where(seq < 31, signal_halo[:, cols], jnp.zeros((TAPS, TILE), BF16))
            spec = signal_spec[:, cols] + spectrum(LATE_HALO, halo)
            real, imag = spec[:HALF], spec[HALF:]
            tap_real, tap_imag = tap_spec[pl.ds(0, HALF), cols], tap_spec[pl.ds(HALF, HALF), cols]
            back = restore(
                pl.ds(ROWS, ROWS),
                real * tap_real + imag * tap_imag,
                imag * tap_real - real * tap_imag,
            )
            made_key[:, cols] = (back * value[:, cols].astype(F32)).astype(BF16)
            made_value[:, cols] = (back * key[:, cols].astype(F32)).astype(BF16)

    finish(y[0] * 2 + odd, "here")
    finish((1 - y[0]) * 2 + odd, "beside")
    from_corner[1][0].wait_recv()
    share_core("corner", 1)
    finish(y[0] * 2 + 1 - odd, "above")
    finish((1 - y[0]) * 2 + 1 - odd, "corner")

    near_sums = gather(near_land)
    for i in range(1, 8):
        send(lag_sum.at[members[i]], near_land.at[i - 1], to_member(members[i]), near_sums, 0)

    combine_all(0, 0)
    combine_all(0, 1)
    near_sums[0].wait_recv()
    total = lag_sum[member].astype(F32)
    for i in range(7):
        total = total + near_land[i].astype(F32)
    lag_mid[...] = total.reshape(8, 16, TAPS)
    far_sums = gather(far_land)
    for i in range(1, 8):
        send(lag_mid.at[heights[i]], far_land.at[i - 1], place(y, heights[i], core), far_sums, 1)

    combine_all(1, 0)
    signal_sent[0].wait_recv()

    restore_back(0)
    combine_all(1, 1)
    combine_all(2, 0)
    far_sums[0].wait_recv()
    total = lag_mid[z]
    for i in range(7):
        total = total + far_land[i]
    lag_out[member, z] = (total * scale).astype(BF16)
    mine = lag_out.at[member, z]
    copies = [send(mine, mine, place(y, heights[i], core), None, 2) for i in range(1, 8)]
    restore_back(2)
    combine_all(2, 1)
    combine_all(3, 0)
    for copy in copies:
        copy.wait_recv()
    mine = lag_out.at[member]
    copies = [send(mine, mine, to_member(members[i]), None, 3) for i in range(1, 8)]
    combine_all(3, 1)
    combine_all(4, 0)
    for copy in copies:
        copy.wait_recv()
    made_filter[...] = lag_out[...].astype(F32)
    diagonal = lax.broadcasted_iota(jnp.int32, (128, 128), 0) == lax.broadcasted_iota(
        jnp.int32, (128, 128), 1
    )
    for i in range(8):
        first_lag = made_filter[i].reshape(128, TAPS)[:, 0:1]
        spread = jnp.where(diagonal, jnp.broadcast_to(first_lag, (128, 128)), 0.0)
        made_skip[pl.ds(i, 1)] = jnp.sum(spread, axis=0, keepdims=True)
    combine_all(4, 1)
    sent = [near_land, far_land, near_land.at[:, pl.ds(0, 16)], near_land]
    for size in started:
        planes = planes_of(size)
        sent.append(full_weight.at[pl.ds(0, planes), pl.ds(0, size // 2048 // planes)])
    for out_number, block in enumerate(sent):
        describe(block, block, to_core, 0, out_number).wait_send()


def hand_on(*refs):
    count = (len(refs) - 1) // 2
    copies = [
        pltpu.make_async_copy(refs[i], refs[count + i], refs[-1].at[i]) for i in range(count)
    ]
    for copy in copies:
        copy.start()
    for copy in copies:
        copy.wait()


def per_device(query_gate, key_gate, value_input, filter_taps, skip_gain, out_weight, cotangent):
    ahead, behind = spectrum_tables()
    anywhere = pl.BlockSpec(memory_space=pl.ANY)
    block = ((ROWS, CHANNELS), BF16)
    scratch = [
        block,
        block,
        block,
        ((CHANNELS, TAPS), BF16),
        ((1, CHANNELS), F32),
        (ahead.shape, BF16),
        (behind.shape, BF16),
        ((4, ROWS, 1024), BF16),
        ((4, CHANNELS, 1024), BF16),
        ((16, 128, 2 * ROWS), BF16),
        ((16, 128, ROWS), BF16),
        ((2 * ROWS, CHANNELS), BF16),
        block,
        ((TAPS, CHANNELS), BF16),
        block,
        ((TAPS, CHANNELS), BF16),
        ((SIZE, CHANNELS), F32),
        ((SIZE, CHANNELS), F32),
        ((SIZE, CHANNELS), F32),
        ((ROWS, CHANNELS), F32),
        ((ROWS, CHANNELS), F32),
        ((4, 2, 8, 2, 64, TILE), BF16),
        ((8, 128, TAPS), BF16),
        ((8, 8, 16, TAPS), BF16),
        ((7, 128, TAPS), BF16),
        ((8, 16, TAPS), F32),
        ((7, 16, TAPS), F32),
    ]
    results = pl.pallas_call(
        kernel,
        out_shape=[
            pltpu.VMEM((ROWS, CHANNELS), BF16),
            pltpu.VMEM((ROWS, CHANNELS), BF16),
            pltpu.VMEM((ROWS, CHANNELS), BF16),
            pltpu.VMEM((8, 8, 16, TAPS), F32),
            pltpu.VMEM((8, 128), F32),
            pltpu.VMEM((64, CHANNELS), F32),
        ],
        in_specs=[anywhere] * 9,
        out_specs=[pl.BlockSpec(memory_space=pltpu.VMEM)] * 6,
        scratch_shapes=[pltpu.VMEM(shape, dtype) for shape, dtype in scratch]
        + [
            pltpu.SemaphoreType.DMA((OUT_EXTRA + OUT_SETS,)),
            pltpu.SemaphoreType.DMA((COPIES,)),
            pltpu.SemaphoreType.DMA((10,)),
        ]
        + [pltpu.VMEM(shape, BF16) for shape in landing_shapes()],
        compiler_params=pltpu.CompilerParams(
            collective_id=0, has_side_effects=True, vmem_limit_bytes=56 * 1024 * 1024
        ),
    )(
        query_gate[0], key_gate[0], value_input[0], filter_taps, skip_gain[None, :],
        out_weight, cotangent[0], jnp.asarray(ahead), jnp.asarray(behind),
    )
    results = [
        results[0][None],
        results[1][None],
        results[2][None],
        results[3].reshape(CHANNELS, TAPS),
        results[4].reshape(CHANNELS),
        results[5],
    ]
    return tuple(
        pl.pallas_call(
            hand_on,
            out_shape=[jax.ShapeDtypeStruct(x.shape, x.dtype) for x in results],
            in_specs=[pl.BlockSpec(memory_space=pltpu.VMEM)] * 6,
            out_specs=[anywhere] * 6,
            scratch_shapes=[pltpu.SemaphoreType.DMA((6,))],
        )(*[pltpu.with_memory_space_constraint(x, pltpu.VMEM) for x in results])
    )


def solution(mesh):
    return jax.shard_map(
        per_device,
        mesh=mesh,
        in_specs=(
            P("dp", "seq", "tp"),
            P("dp", "seq", "tp"),
            P("dp", "seq", "tp"),
            P("tp", None),
            P("tp"),
            P("tp", "dp"),
            P("dp", "seq", "tp"),
        ),
        out_specs=(
            P("dp", "seq", "tp"),
            P("dp", "seq", "tp"),
            P("dp", "seq", "tp"),
            P("tp", None),
            P("tp"),
            P(("seq", "dp"), "tp"),
        ),
        check_vma=False,
    )
```

```python
import itertools
import math

import jax
import jax.numpy as jnp
import ml_dtypes
import numpy as np
from jax import lax
from jax.experimental import pallas as pl
from jax.experimental.pallas import tpu as pltpu
from jax.sharding import PartitionSpec as P

ROWS = 256
TAPS = 128
SIZE = ROWS + TAPS
HALF = SIZE // 2
CHANNELS = 1024
TILE = 256
STREAMS = 2
LANES = TILE // STREAMS
PER_QUARTER = 5 * STREAMS
SENT_ROWS = 2048
OUT_EXTRA, OUT_SETS = 4, 3
COPIES = 96
BF16 = jnp.bfloat16
F32 = jnp.float32


PARTS = ((TAPS, ROWS), (0, TAPS), (0, ROWS), (ROWS, TAPS))
LATE_BLOCK, EARLY_HALO, EARLY_BLOCK, LATE_HALO = 0, 2 * ROWS, 2 * SIZE, 2 * SIZE + 2 * ROWS


def split_table(table):
    high = table.astype(ml_dtypes.bfloat16)
    return high, (table - high.astype(np.float64)).astype(ml_dtypes.bfloat16)


def spectrum_tables():
    odd = 2 * np.arange(HALF) + 1

    def angles(positions):
        return np.pi * ((odd[:, None] * positions[None, :]) % (2 * SIZE)) / SIZE

    ahead = angles(np.arange(SIZE))
    forward = np.concatenate([np.cos(ahead), -np.sin(ahead)], axis=0)
    places = np.concatenate(
        [np.arange(TAPS, SIZE), np.arange(ROWS), np.arange(-TAPS, 0)]
    )
    behind = angles(places).T
    inverse = (2.0 / SIZE) * np.concatenate([np.cos(behind), -np.sin(behind)], axis=1)
    high, low = split_table(forward)
    pieces = [piece[:, start : start + size] for start, size in PARTS for piece in (high, low)]
    back_high, back_low = split_table(inverse)
    return (
        np.concatenate(pieces, axis=1),
        np.concatenate([back_high, back_low, back_high], axis=1),
    )


def matmul(left, right):
    return jnp.dot(left, right, preferred_element_type=F32)


def matmul_nt(left, right):
    return lax.dot_general(
        left, right, (((1,), (1,)), ((), ())), preferred_element_type=F32
    )


def y_near(y):
    return (1 - y[0], y[1])


def y_far(y):
    return (1 - y[0], 1 - y[1])


def z_up(z):
    return z + 1 - 2 * lax.rem(z, 2)


def z_down(z):
    return lax.rem(z + 2 * lax.rem(z, 2) + 7, 8)


def z_three(z):
    return lax.rem(z + 11 - 6 * lax.rem(z, 2), 8)


def z_back_three(z):
    return lax.rem(z + 5 + 6 * lax.rem(z, 2), 8)


PLANS = (
    (("y", y_near), ("y", y_far), ("z", z_up), ("z", z_down), ("z", z_three)),
    (("y", y_far), ("y", y_near), ("z", z_down), ("z", z_up), ("z", z_back_three)),
    (("z", z_up), ("z", z_down), ("y", y_near), ("y", y_far), ("z", z_three)),
    (("z", z_down), ("z", z_up), ("y", y_far), ("y", y_near), ("z", z_back_three)),
)


def kept(rest, place):
    if not rest:
        return [place]
    return kept(rest[1:], place) + kept(rest[1:], rest[0](place))


def remaining(plan, step, axis):
    return [move for name, move in plan[step + 1 :] if name == axis]


def slots(plan, step, y, z):
    y_rest, z_rest = remaining(plan, step, "y"), remaining(plan, step, "z")
    y_list = [None] if len(y_rest) == 2 else kept(y_rest, y)
    z_list = [None] if len(z_rest) == 3 else kept(z_rest, z)
    return [(one, other) for one in y_list for other in z_list]


def slot_view(ref, quarter, slot, lanes):
    y, z = slot
    if y is None:
        return ref.at[quarter, :, z, :, :, lanes]
    if z is None:
        return ref.at[quarter, y[0], :, y[1], :, lanes]
    return ref.at[quarter, y[0], z, y[1], :, lanes]


def planes_of(size):
    for planes in range(1, 5):
        if size % (2048 * 16 * planes) == 0 and size // (2048 * planes) <= 1024:
            return planes
    return None


def landing_shapes():
    shapes = []
    for plan in PLANS:
        shapes += [(4, 4, 64, LANES) if plan[0][0] == "y" else (4, 2, 2, 64, LANES)] * STREAMS
        for step in range(1, 5):
            y_rest, z_rest = remaining(plan, step, "y"), remaining(plan, step, "z")
            if len(y_rest) == 2:
                shape = (2 ** len(z_rest), 2, 2, 64, LANES)
            elif len(z_rest) == 3:
                shape = (2 ** len(y_rest), 8, 64, LANES)
            else:
                shape = (2 ** (len(y_rest) + len(z_rest)), 64, LANES)
            shapes += [shape] * STREAMS
    return shapes


def first_slots(quarter, owner, y, z, keep):
    low, half = lax.div(owner, 2), lax.rem(owner, 2)
    group = pl.ds(half * 4, 4)
    other = 0 if keep else 1
    if quarter == 0:
        return [(low, group, lax.rem(y[1] + y[0] + low + other, 2))]
    if quarter == 1:
        return [(low, group, lax.rem(y[1] + other, 2))]
    if quarter == 2:
        kind = lax.rem(lax.div(lax.rem(z, 4) + 1, 2) + other, 2)
        return [(low, half * 4 + kind + i * (3 - 2 * kind)) for i in range(2)]
    kind = lax.rem(lax.div(lax.rem(z, 4), 2) + other, 2)
    return [(low, half * 4 + kind * 2 + i) for i in range(2)]


def kernel(
    query_in, key_in, value_in, taps_in, skip_in, weight, cot, ahead_in, behind_in,
    made_query, made_key, made_value, made_filter, made_skip, made_weight,
    query, key, value, taps, skip, ahead, behind,
    full_cot, full_weight, turned, turned_away, gated, mixed, mixed_halo, signal, signal_halo,
    tap_spec, mixed_spec, signal_spec, state, grad_gated, partial, lag_sum, lag_out,
    near_land, lag_mid, far_land, send_sem, recv_sem, local_sem, *landing,
):
    seq, tp, dp = lax.axis_index("seq"), lax.axis_index("tp"), lax.axis_index("dp")
    core = lax.rem(seq, 2)
    z = lax.rem(lax.div(seq, 2), 8)
    y = (lax.div(seq, 16), dp)
    scale = 1.0 / math.sqrt(2 * 32 * ROWS)

    def place(y, z, core):
        return ((y[0] * 8 + z) * 2 + core, tp, y[1])

    right, left, across = lax.rem(tp + 1, 4), lax.rem(tp + 3, 4), lax.rem(tp + 2, 4)
    to_right, to_left = (seq, right, dp), (seq, left, dp)
    to_next, to_prior = (lax.rem(seq + 1, 32), tp, dp), (lax.rem(seq + 31, 32), tp, dp)
    to_core = place(y, z, 1 - core)
    to_near, to_far = place(y_near(y), z, core), place(y_far(y), z, core)
    to_side = [place(y, z_up(z), core), place(y, z_down(z), core)]
    member = (y[1] * 2 + y[0]) * 2 + core

    def to_member(index):
        high = lax.div(index, 4)
        return place((lax.rem(lax.div(index, 2), 2), high), z, lax.rem(index, 2))

    members = [lax.rem(member + i, 8) for i in range(8)]
    heights = [lax.rem(z + i, 8) for i in range(8)]

    barrier = pltpu.get_barrier_semaphore()
    greeted = [to_right, to_left, to_next, to_prior]
    greeted += [to_member(members[i]) for i in range(1, 8)]
    greeted += [place(y, heights[i], core) for i in range(1, 8)]
    for target in greeted:
        pl.semaphore_signal(
            barrier, inc=1, device_id=target, device_id_type=pl.DeviceIdType.MESH
        )

    local_numbers = itertools.count()

    def fetch(source, target):
        copy = pltpu.make_async_copy(source, target, local_sem.at[next(local_numbers)])
        copy.start()
        return copy

    key_copy, value_copy = fetch(key_in, key), fetch(value_in, value)
    cot_copy = fetch(cot, full_cot.at[tp])
    table_copies = [fetch(ahead_in, ahead), fetch(taps_in, taps), fetch(skip_in, skip)]
    state_copies = [fetch(behind_in, behind), fetch(query_in, query)]
    key_copy.wait()
    value_copy.wait()
    mixed[...] = (key[...].astype(F32) * value[...].astype(F32)).astype(BF16)
    pl.semaphore_wait(barrier, len(greeted))

    numbers = itertools.count()
    started = []

    def describe(source, target_ref, target, number, out_number):
        return pltpu.make_async_remote_copy(
            src_ref=source,
            dst_ref=target_ref,
            send_sem=send_sem.at[out_number],
            recv_sem=recv_sem.at[number],
            device_id=target,
            device_id_type=pl.DeviceIdType.MESH,
        )

    def send(source, target_ref, target, group=None, out=None):
        size = math.prod(source.shape) * source.dtype.itemsize
        if out is None:
            if not started or started[-1] >= SENT_ROWS * 2048 and planes_of(started[-1]):
                started.append(0)
            started[-1] += size
        number = next(numbers) if group is None else group[1]
        out_number = OUT_EXTRA + len(started) - 1 if out is None else out
        copy = describe(source, target_ref, target, number, out_number)
        copy.start()
        return copy

    def gather(landed):
        number = next(numbers)
        return describe(landed, landed, to_core, number, 0), number

    top, bottom = pl.ds(0, 128), pl.ds(128, 128)

    def pass_cot(owner, part, target):
        spot = full_cot.at[owner, part]
        return send(spot, spot, target)

    right_top = send(cot.at[top], full_cot.at[tp, top], to_right)
    left_bottom = send(cot.at[bottom], full_cot.at[tp, bottom], to_left)

    def weight_rows(low, odd, core):
        return pl.ds(pl.multiple_of(((low * 2 + odd) * 2 + core) * 128, 128), 128)

    odd = lax.rem(z, 2)
    given = weight_rows(1 - y[0], odd, core)
    imports = []
    for i in range(2):
        for r in range(4):
            rows = pl.ds(pl.multiple_of(given.start + r * 32, 32), 32)
            source = weight.at[rows, pl.ds(i * 1024, 1024)]
            imports.append(send(source, full_weight.at[dp * 2 + i, rows], to_far))
    right_bottom = send(cot.at[bottom], full_cot.at[tp, bottom], to_right)
    left_top = send(cot.at[top], full_cot.at[tp, top], to_left)
    own = [fetch(weight.at[:, pl.ds(i * 1024, 1024)], full_weight.at[dp * 2 + i]) for i in range(2)]

    wide = [pl.ds(h * 2 * TILE, 2 * TILE) for h in range(2)]
    mixed_sent = [send(mixed.at[bottom, cols], mixed_halo.at[:, cols], to_next) for cols in wide]

    def turn(owner, start, size):
        tokens, far_tokens = pl.ds(start, size), pl.ds(ROWS + start, size)
        for i in range(4):
            mine = pl.ds(pl.multiple_of((i * 2 + core) * 128, 128), 128)
            other = pl.ds(pl.multiple_of((i * 2 + 1 - core) * 128, 128), 128)
            turned[owner * 4 + i, :, tokens] = full_cot[owner, tokens, mine].T
            turned_away[owner * 4 + i, :, tokens] = full_cot[owner, tokens, other].T
        group = pl.ds(owner * 4, 4)
        return send(turned_away.at[group, :, tokens], turned.at[group, :, far_tokens], to_core)

    cot_copy.wait()
    turned_own = turn(tp, 0, ROWS)

    def columns(tile):
        return pl.ds(pl.multiple_of(tile * TILE, TILE), TILE)

    def spectrum(start, block):
        table = ahead[:, pl.ds(start, 2 * block.shape[0])]
        return matmul(table, jnp.concatenate([block, block], axis=0))

    def restore(places, real, imag):
        spec = jnp.concatenate([real, imag], axis=0)
        high = spec.astype(BF16)
        low = (spec - high.astype(F32)).astype(BF16)
        return matmul(behind[places], jnp.concatenate([high, high, low], axis=0))

    for copy in table_copies:
        copy.wait()

    @pl.loop(0, CHANNELS // TILE)
    def _(tile):
        cols = columns(tile)
        block = taps[cols]
        table = ahead[:, pl.ds(EARLY_HALO, 2 * TAPS)]
        spec = matmul_nt(table, jnp.concatenate([block, block], axis=1))
        tap_spec[pl.ds(0, HALF), cols] = spec[:HALF] + skip[:, cols]
        tap_spec[pl.ds(HALF, HALF), cols] = spec[HALF:]
        mixed_spec[:, cols] = spectrum(LATE_BLOCK, mixed[:, cols])

    def block_rows(kind, core):
        low = y[0] if kind in ("here", "above") else 1 - y[0]
        return weight_rows(low, odd if kind in ("here", "beside") else 1 - odd, core)

    kinds = ("here", "beside", "above", "corner")
    others = pl.ds((1 - dp) * 2, 2)
    from_core = {kind: gather(full_weight.at[others, block_rows(kind, 1 - core)]) for kind in kinds}
    from_side = gather(full_weight.at[others, block_rows("above", core)])
    from_corner = [
        gather(full_weight.at[(1 - dp) * 2 + i, block_rows("corner", core)]) for i in range(2)
    ]
    near_copies = []

    def weight_spot(kind, number):
        part = pl.ds(pl.multiple_of(block_rows(kind, core).start + number % 4 * 32, 32), 32)
        return full_weight.at[(1 - dp) * 2 + number // 4, part]

    def share_core(kind, i):
        spot = full_weight.at[(1 - dp) * 2 + i, block_rows(kind, core)]
        send(spot, spot, to_core, from_core[kind])

    def share_import(number):
        imports[number].wait_recv()
        spot = weight_spot("here", number)
        near_copies.append(send(spot, spot, to_near))
        send(spot, spot, to_side[number % 2], from_side)
        if number % 4 == 3:
            share_core("here", number // 4)

    def share_near(number):
        near_copies[number].wait_recv()
        spot = weight_spot("beside", number)
        send(spot, spot, to_side[number % 2], from_corner[number // 4])
        if number % 4 == 3:
            share_core("beside", number // 4)

    def convolve(start):
        @pl.loop(start, start + 2)
        def _(tile):
            cols = columns(tile)
            halo = jnp.where(seq > 0, mixed_halo[:, cols], jnp.zeros((TAPS, TILE), BF16))
            spec = mixed_spec[:, cols] + spectrum(EARLY_HALO, halo)
            mixed_spec[:, cols] = spec
            real, imag = spec[:HALF], spec[HALF:]
            tap_real, tap_imag = tap_spec[pl.ds(0, HALF), cols], tap_spec[pl.ds(HALF, HALF), cols]
            value_now = restore(
                pl.ds(0, ROWS),
                real * tap_real - imag * tap_imag,
                real * tap_imag + imag * tap_real,
            )
            state[:, cols] = value_now
            gated[pl.ds(0, ROWS), cols] = (query[:, cols].astype(F32) * value_now).astype(BF16)

    for copy in state_copies:
        copy.wait()
    gated_sent = []
    for h in range(2):
        mixed_sent[h].wait_recv()
        convolve(2 * h)
        half = gated.at[pl.ds(0, ROWS), wide[h]]
        gated_sent.append(send(half, gated.at[pl.ds(ROWS, ROWS), wide[h]], to_core))

    first = [
        [gather(landing[quarter * PER_QUARTER + stream]) for stream in range(STREAMS)]
        for quarter in range(4)
    ]

    def lanes_of(stream):
        return pl.ds(stream * LANES, LANES)

    def first_view(quarter, slot, stream):
        if quarter < 2:
            return partial.at[quarter, slot[0], slot[1], slot[2], :, lanes_of(stream)]
        return partial.at[quarter, slot[0], slot[1], :, :, lanes_of(stream)]

    def first_landing(quarter, chunk, i, stream):
        landed = landing[quarter * PER_QUARTER + stream]
        return landed.at[chunk] if quarter < 2 else landed.at[chunk, i]

    first_targets = [to_near, to_far, to_side[0], to_side[1]]

    def products(owner, start=0, stop=4):
        low, group = lax.div(owner, 2), pl.ds(lax.rem(owner, 2) * 4, 4)

        @pl.loop(start, stop)
        def _(quarter):
            rows = turned[pl.ds(owner * 4, 4)].reshape(512, 2 * ROWS)
            block = matmul(rows, gated[:, columns(quarter)]).astype(BF16)
            partial[quarter, low, group] = block.reshape(4, 2, 64, TILE)

    def halve(chunk, owner, stream, quarters=(0, 1, 2, 3)):
        for quarter in quarters:
            for i, slot in enumerate(first_slots(quarter, owner, y, z, False)):
                send(
                    first_view(quarter, slot, stream),
                    first_landing(quarter, chunk, i, stream),
                    first_targets[quarter],
                    first[quarter][stream],
                )

    share_import(0)
    share_import(1)
    turned_own.wait_recv()
    gated_sent[0].wait_recv()
    products(tp, 0, 2)
    halve(0, tp, 0, (0, 1))
    halve(0, tp, 1, (1,))
    share_import(2)
    gated_sent[1].wait_recv()
    products(tp, 2, 4)
    for stream in range(STREAMS):
        halve(0, tp, stream, (2, 3))
    right_top.wait_recv()
    forward_right = pass_cot(left, top, to_right)
    left_bottom.wait_recv()
    forward_left = pass_cot(right, bottom, to_left)
    share_import(3)
    share_near(0)
    turned_left = [turn(left, 0, 128)]
    turned_right = [turn(right, 128, 128)]
    share_import(4)
    share_import(5)
    share_import(6)
    right_bottom.wait_recv()
    turned_left.append(turn(left, 128, 128))
    left_top.wait_recv()
    turned_right.append(turn(right, 0, 128))
    share_import(7)
    share_near(1)
    share_near(2)
    for copy in own:
        copy.wait()
    late = jnp.where(lax.div(across, 2) == dp, across, dp * 4 + 1 - tp)
    early = dp * 4 + 1 - late

    @pl.loop(0, CHANNELS // TILE)
    def _(tile):
        cols = columns(tile)
        grad_gated[:, cols] = matmul_nt(full_cot[early], full_weight[early, cols])

    share_near(3)
    for copy in turned_left:
        copy.wait_recv()
    products(left)
    halve(1, left, 0)
    share_near(4)
    share_near(5)
    for copy in turned_right:
        copy.wait_recv()
    products(right)
    halve(2, right, 0)
    forward_right.wait_recv()
    forward_left.wait_recv()
    turned_across = turn(across, 0, ROWS)
    share_near(6)
    share_near(7)
    halve(0, tp, 1, (0,))
    halve(1, left, 1)
    @pl.loop(0, CHANNELS // TILE)
    def _(tile):
        cols = columns(tile)
        grad_gated[:, cols] += matmul_nt(full_cot[late], full_weight[late, cols])

    turned_across.wait_recv()
    products(across)
    halve(3, across, 0)
    halve(2, right, 1)
    halve(3, across, 1)

    from_side[0].wait_recv()
    share_core("above", 0)
    share_core("above", 1)
    from_corner[0][0].wait_recv()
    share_core("corner", 0)
    signal_sent = gather(signal_halo)
    near_sums = gather(near_land)

    def finish(tile, kind):
        from_core[kind][0].wait_recv()
        cols = columns(tile)
        total = grad_gated[:, cols]
        for i in range(2):
            owner = (1 - dp) * 2 + i
            total = total + matmul_nt(full_cot[owner], full_weight[owner, cols])
        made_query[:, cols] = (total * state[:, cols]).astype(BF16)
        signal[:, cols] = (total * query[:, cols].astype(F32)).astype(BF16)
        send(signal.at[top, cols], signal_halo.at[:, cols], to_prior, signal_sent)
        spec = spectrum(EARLY_BLOCK, signal[:, cols])
        signal_spec[:, cols] = spec
        real, imag = spec[:HALF], spec[HALF:]
        part_real, part_imag = mixed_spec[pl.ds(0, HALF), cols], mixed_spec[pl.ds(HALF, HALF), cols]
        lags = restore(
            pl.ds(2 * ROWS, TAPS),
            real * part_real + imag * part_imag,
            imag * part_real - real * part_imag,
        )
        for i in range(TILE // 128):
            block = lags[:, i * 128 : (i + 1) * 128].T
            owner = tile * 2 + i
            ahead_by = lax.rem(owner + 8 - member, 8)
            lag_sum[owner] = block.astype(BF16)

            @pl.when(ahead_by > 0)
            def _():
                send(
                    lag_sum.at[owner], near_land.at[ahead_by - 1], to_member(owner), near_sums, 0
                )


    rounds = {}

    def exchange(quarter, step, stream):
        axis, move = PLANS[quarter][step]
        there_y = move(y) if axis == "y" else y
        there_z = move(z) if axis == "z" else z
        landed = landing[quarter * PER_QUARTER + step * STREAMS + stream]
        group = gather(landed)
        for i, slot in enumerate(slots(PLANS[quarter], step, there_y, there_z)):
            view = slot_view(partial, quarter, slot, lanes_of(stream))
            send(view, landed.at[i], place(there_y, there_z, core), group)
        rounds[quarter, step, stream] = group[0], landed

    def combine(quarter, step, stream):
        lanes = lanes_of(stream)
        if step == 0:
            first[quarter][stream][0].wait_recv()
            pairs = [
                (first_view(quarter, slot, stream), first_landing(quarter, chunk, i, stream))
                for chunk, owner in enumerate((tp, left, right, across))
                for i, slot in enumerate(first_slots(quarter, owner, y, z, True))
            ]
        else:
            copy, landed = rounds[quarter, step, stream]
            copy.wait_recv()
            pairs = [
                (slot_view(partial, quarter, slot, lanes), landed.at[i])
                for i, slot in enumerate(slots(PLANS[quarter], step, y, z))
            ]
        for view, landed in pairs:
            total = view[...].astype(F32) + landed[...].astype(F32)
            if step < 4:
                view[...] = total.astype(BF16)
            else:
                place_out = pl.ds(quarter * TILE + stream * LANES, LANES)
                made_weight[:, place_out] = total * scale
        if step < 4:
            exchange(quarter, step + 1, stream)

    def combine_all(step, stream):
        for quarter in range(4):
            combine(quarter, step, stream)

    def restore_back(start):
        @pl.loop(start, start + 2)
        def _(tile):
            cols = columns(tile)
            halo = jnp.where(seq < 31, signal_halo[:, cols], jnp.zeros((TAPS, TILE), BF16))
            spec = signal_spec[:, cols] + spectrum(LATE_HALO, halo)
            real, imag = spec[:HALF], spec[HALF:]
            tap_real, tap_imag = tap_spec[pl.ds(0, HALF), cols], tap_spec[pl.ds(HALF, HALF), cols]
            back = restore(
                pl.ds(ROWS, ROWS),
                real * tap_real + imag * tap_imag,
                imag * tap_real - real * tap_imag,
            )
            made_key[:, cols] = (back * value[:, cols].astype(F32)).astype(BF16)
            made_value[:, cols] = (back * key[:, cols].astype(F32)).astype(BF16)

    finish(y[0] * 2 + odd, "here")
    finish((1 - y[0]) * 2 + odd, "beside")
    combine_all(0, 0)
    from_corner[1][0].wait_recv()
    share_core("corner", 1)
    finish(y[0] * 2 + 1 - odd, "above")
    finish((1 - y[0]) * 2 + 1 - odd, "corner")

    combine_all(0, 1)
    combine_all(1, 0)
    near_sums[0].wait_recv()
    total = lag_sum[member].astype(F32)
    for i in range(7):
        total = total + near_land[i].astype(F32)
    lag_mid[...] = total.reshape(8, 16, TAPS)
    far_sums = gather(far_land)
    for i in range(1, 8):
        send(lag_mid.at[heights[i]], far_land.at[i - 1], place(y, heights[i], core), far_sums, 1)

    signal_sent[0].wait_recv()

    restore_back(0)
    combine_all(1, 1)
    combine_all(2, 0)
    far_sums[0].wait_recv()
    total = lag_mid[z]
    for i in range(7):
        total = total + far_land[i]
    lag_out[member, z] = (total * scale).astype(BF16)
    mine = lag_out.at[member, z]
    copies = [send(mine, mine, place(y, heights[i], core), None, 2) for i in range(1, 8)]
    restore_back(2)
    combine_all(2, 1)
    combine_all(3, 0)
    for copy in copies:
        copy.wait_recv()
    mine = lag_out.at[member]
    copies = [send(mine, mine, to_member(members[i]), None, 3) for i in range(1, 8)]
    combine_all(3, 1)
    combine_all(4, 0)
    for copy in copies:
        copy.wait_recv()
    made_filter[...] = lag_out[...].astype(F32)
    diagonal = lax.broadcasted_iota(jnp.int32, (128, 128), 0) == lax.broadcasted_iota(
        jnp.int32, (128, 128), 1
    )
    for i in range(8):
        first_lag = made_filter[i].reshape(128, TAPS)[:, 0:1]
        spread = jnp.where(diagonal, jnp.broadcast_to(first_lag, (128, 128)), 0.0)
        made_skip[pl.ds(i, 1)] = jnp.sum(spread, axis=0, keepdims=True)
    combine_all(4, 1)
    sent = [near_land, far_land, near_land.at[:, pl.ds(0, 16)], near_land]
    for size in started:
        planes = planes_of(size)
        sent.append(full_weight.at[pl.ds(0, planes), pl.ds(0, size // 2048 // planes)])
    for out_number, block in enumerate(sent):
        describe(block, block, to_core, 0, out_number).wait_send()


def hand_on(*refs):
    count = (len(refs) - 1) // 2
    copies = [
        pltpu.make_async_copy(refs[i], refs[count + i], refs[-1].at[i]) for i in range(count)
    ]
    for copy in copies:
        copy.start()
    for copy in copies:
        copy.wait()


def per_device(query_gate, key_gate, value_input, filter_taps, skip_gain, out_weight, cotangent):
    ahead, behind = spectrum_tables()
    anywhere = pl.BlockSpec(memory_space=pl.ANY)
    block = ((ROWS, CHANNELS), BF16)
    scratch = [
        block,
        block,
        block,
        ((CHANNELS, TAPS), BF16),
        ((1, CHANNELS), F32),
        (ahead.shape, BF16),
        (behind.shape, BF16),
        ((4, ROWS, 1024), BF16),
        ((4, CHANNELS, 1024), BF16),
        ((16, 128, 2 * ROWS), BF16),
        ((16, 128, ROWS), BF16),
        ((2 * ROWS, CHANNELS), BF16),
        block,
        ((TAPS, CHANNELS), BF16),
        block,
        ((TAPS, CHANNELS), BF16),
        ((SIZE, CHANNELS), F32),
        ((SIZE, CHANNELS), F32),
        ((SIZE, CHANNELS), F32),
        ((ROWS, CHANNELS), F32),
        ((ROWS, CHANNELS), F32),
        ((4, 2, 8, 2, 64, TILE), BF16),
        ((8, 128, TAPS), BF16),
        ((8, 8, 16, TAPS), BF16),
        ((7, 128, TAPS), BF16),
        ((8, 16, TAPS), F32),
        ((7, 16, TAPS), F32),
    ]
    results = pl.pallas_call(
        kernel,
        out_shape=[
            pltpu.VMEM((ROWS, CHANNELS), BF16),
            pltpu.VMEM((ROWS, CHANNELS), BF16),
            pltpu.VMEM((ROWS, CHANNELS), BF16),
            pltpu.VMEM((8, 8, 16, TAPS), F32),
            pltpu.VMEM((8, 128), F32),
            pltpu.VMEM((64, CHANNELS), F32),
        ],
        in_specs=[anywhere] * 9,
        out_specs=[pl.BlockSpec(memory_space=pltpu.VMEM)] * 6,
        scratch_shapes=[pltpu.VMEM(shape, dtype) for shape, dtype in scratch]
        + [
            pltpu.SemaphoreType.DMA((OUT_EXTRA + OUT_SETS,)),
            pltpu.SemaphoreType.DMA((COPIES,)),
            pltpu.SemaphoreType.DMA((10,)),
        ]
        + [pltpu.VMEM(shape, BF16) for shape in landing_shapes()],
        compiler_params=pltpu.CompilerParams(
            collective_id=0, has_side_effects=True, vmem_limit_bytes=56 * 1024 * 1024
        ),
    )(
        query_gate[0], key_gate[0], value_input[0], filter_taps, skip_gain[None, :],
        out_weight, cotangent[0], jnp.asarray(ahead), jnp.asarray(behind),
    )
    results = [
        results[0][None],
        results[1][None],
        results[2][None],
        results[3].reshape(CHANNELS, TAPS),
        results[4].reshape(CHANNELS),
        results[5],
    ]
    return tuple(
        pl.pallas_call(
            hand_on,
            out_shape=[jax.ShapeDtypeStruct(x.shape, x.dtype) for x in results],
            in_specs=[pl.BlockSpec(memory_space=pltpu.VMEM)] * 6,
            out_specs=[anywhere] * 6,
            scratch_shapes=[pltpu.SemaphoreType.DMA((6,))],
        )(*[pltpu.with_memory_space_constraint(x, pltpu.VMEM) for x in results])
    )


def solution(mesh):
    return jax.shard_map(
        per_device,
        mesh=mesh,
        in_specs=(
            P("dp", "seq", "tp"),
            P("dp", "seq", "tp"),
            P("dp", "seq", "tp"),
            P("tp", None),
            P("tp"),
            P("tp", "dp"),
            P("dp", "seq", "tp"),
        ),
        out_specs=(
            P("dp", "seq", "tp"),
            P("dp", "seq", "tp"),
            P("dp", "seq", "tp"),
            P("tp", None),
            P("tp"),
            P(("seq", "dp"), "tp"),
        ),
        check_vma=False,
    )
```

```python
import itertools
import math

import jax
import jax.numpy as jnp
import ml_dtypes
import numpy as np
from jax import lax
from jax.experimental import pallas as pl
from jax.experimental.pallas import tpu as pltpu
from jax.sharding import PartitionSpec as P

ROWS = 256
TAPS = 128
SIZE = ROWS + TAPS
HALF = SIZE // 2
CHANNELS = 1024
TILE = 256
STREAMS = 2
LANES = TILE // STREAMS
PER_QUARTER = 5 * STREAMS
SENT_ROWS = 2048
OUT_EXTRA, OUT_SETS = 4, 3
COPIES = 96
BF16 = jnp.bfloat16
F32 = jnp.float32


PARTS = ((TAPS, ROWS), (0, TAPS), (0, ROWS), (ROWS, TAPS))
LATE_BLOCK, EARLY_HALO, EARLY_BLOCK, LATE_HALO = 0, 2 * ROWS, 2 * SIZE, 2 * SIZE + 2 * ROWS


def split_table(table):
    high = table.astype(ml_dtypes.bfloat16)
    return high, (table - high.astype(np.float64)).astype(ml_dtypes.bfloat16)


def spectrum_tables():
    odd = 2 * np.arange(HALF) + 1

    def angles(positions):
        return np.pi * ((odd[:, None] * positions[None, :]) % (2 * SIZE)) / SIZE

    ahead = angles(np.arange(SIZE))
    forward = np.concatenate([np.cos(ahead), -np.sin(ahead)], axis=0)
    places = np.concatenate(
        [np.arange(TAPS, SIZE), np.arange(ROWS), np.arange(-TAPS, 0)]
    )
    behind = angles(places).T
    inverse = (2.0 / SIZE) * np.concatenate([np.cos(behind), -np.sin(behind)], axis=1)
    high, low = split_table(forward)
    pieces = [piece[:, start : start + size] for start, size in PARTS for piece in (high, low)]
    back_high, back_low = split_table(inverse)
    return (
        np.concatenate(pieces, axis=1),
        np.concatenate([back_high, back_low, back_high], axis=1),
    )


def matmul(left, right):
    return jnp.dot(left, right, preferred_element_type=F32)


def matmul_nt(left, right):
    return lax.dot_general(
        left, right, (((1,), (1,)), ((), ())), preferred_element_type=F32
    )


def y_near(y):
    return (1 - y[0], y[1])


def y_far(y):
    return (1 - y[0], 1 - y[1])


def z_up(z):
    return z + 1 - 2 * lax.rem(z, 2)


def z_down(z):
    return lax.rem(z + 2 * lax.rem(z, 2) + 7, 8)


def z_three(z):
    return lax.rem(z + 11 - 6 * lax.rem(z, 2), 8)


def z_back_three(z):
    return lax.rem(z + 5 + 6 * lax.rem(z, 2), 8)


PLANS = (
    (("y", y_near), ("y", y_far), ("z", z_up), ("z", z_down), ("z", z_three)),
    (("y", y_far), ("y", y_near), ("z", z_down), ("z", z_up), ("z", z_back_three)),
    (("z", z_up), ("z", z_down), ("y", y_near), ("y", y_far), ("z", z_three)),
    (("z", z_down), ("z", z_up), ("y", y_far), ("y", y_near), ("z", z_back_three)),
)


def kept(rest, place):
    if not rest:
        return [place]
    return kept(rest[1:], place) + kept(rest[1:], rest[0](place))


def remaining(plan, step, axis):
    return [move for name, move in plan[step + 1 :] if name == axis]


def slots(plan, step, y, z):
    y_rest, z_rest = remaining(plan, step, "y"), remaining(plan, step, "z")
    y_list = [None] if len(y_rest) == 2 else kept(y_rest, y)
    z_list = [None] if len(z_rest) == 3 else kept(z_rest, z)
    return [(one, other) for one in y_list for other in z_list]


def slot_view(ref, quarter, slot, lanes):
    y, z = slot
    if y is None:
        return ref.at[quarter, :, z, :, :, lanes]
    if z is None:
        return ref.at[quarter, y[0], :, y[1], :, lanes]
    return ref.at[quarter, y[0], z, y[1], :, lanes]


def planes_of(size):
    for planes in range(1, 5):
        if size % (2048 * 16 * planes) == 0 and size // (2048 * planes) <= 1024:
            return planes
    return None


def landing_shapes():
    shapes = []
    for plan in PLANS:
        shapes += [(4, 4, 64, LANES) if plan[0][0] == "y" else (4, 2, 2, 64, LANES)] * STREAMS
        for step in range(1, 5):
            y_rest, z_rest = remaining(plan, step, "y"), remaining(plan, step, "z")
            if len(y_rest) == 2:
                shape = (2 ** len(z_rest), 2, 2, 64, LANES)
            elif len(z_rest) == 3:
                shape = (2 ** len(y_rest), 8, 64, LANES)
            else:
                shape = (2 ** (len(y_rest) + len(z_rest)), 64, LANES)
            shapes += [shape] * STREAMS
    return shapes


def first_slots(quarter, owner, y, z, keep):
    low, half = lax.div(owner, 2), lax.rem(owner, 2)
    group = pl.ds(half * 4, 4)
    other = 0 if keep else 1
    if quarter == 0:
        return [(low, group, lax.rem(y[1] + y[0] + low + other, 2))]
    if quarter == 1:
        return [(low, group, lax.rem(y[1] + other, 2))]
    if quarter == 2:
        kind = lax.rem(lax.div(lax.rem(z, 4) + 1, 2) + other, 2)
        return [(low, half * 4 + kind + i * (3 - 2 * kind)) for i in range(2)]
    kind = lax.rem(lax.div(lax.rem(z, 4), 2) + other, 2)
    return [(low, half * 4 + kind * 2 + i) for i in range(2)]


def kernel(
    query_in, key_in, value_in, taps_in, skip_in, weight, cot, ahead_in, behind_in,
    made_query, made_key, made_value, made_filter, made_skip, made_weight,
    query, key, value, taps, skip, ahead, behind,
    full_cot, full_weight, turned, turned_away, gated, mixed, mixed_halo, signal, signal_halo,
    tap_spec, mixed_spec, signal_spec, state, grad_gated, partial, lag_sum, lag_out,
    near_land, lag_mid, far_land, send_sem, recv_sem, local_sem, *landing,
):
    seq, tp, dp = lax.axis_index("seq"), lax.axis_index("tp"), lax.axis_index("dp")
    core = lax.rem(seq, 2)
    z = lax.rem(lax.div(seq, 2), 8)
    y = (lax.div(seq, 16), dp)
    scale = 1.0 / math.sqrt(2 * 32 * ROWS)

    def place(y, z, core):
        return ((y[0] * 8 + z) * 2 + core, tp, y[1])

    right, left, across = lax.rem(tp + 1, 4), lax.rem(tp + 3, 4), lax.rem(tp + 2, 4)
    to_right, to_left = (seq, right, dp), (seq, left, dp)
    to_next, to_prior = (lax.rem(seq + 1, 32), tp, dp), (lax.rem(seq + 31, 32), tp, dp)
    to_core = place(y, z, 1 - core)
    to_near, to_far = place(y_near(y), z, core), place(y_far(y), z, core)
    to_side = [place(y, z_up(z), core), place(y, z_down(z), core)]
    member = (y[1] * 2 + y[0]) * 2 + core

    def to_member(index):
        high = lax.div(index, 4)
        return place((lax.rem(lax.div(index, 2), 2), high), z, lax.rem(index, 2))

    members = [lax.rem(member + i, 8) for i in range(8)]
    heights = [lax.rem(z + i, 8) for i in range(8)]

    barrier = pltpu.get_barrier_semaphore()
    greeted = [to_right, to_left, to_next, to_prior]
    greeted += [to_member(members[i]) for i in range(1, 8)]
    greeted += [place(y, heights[i], core) for i in range(1, 8)]
    for target in greeted:
        pl.semaphore_signal(
            barrier, inc=1, device_id=target, device_id_type=pl.DeviceIdType.MESH
        )

    local_numbers = itertools.count()

    def fetch(source, target):
        copy = pltpu.make_async_copy(source, target, local_sem.at[next(local_numbers)])
        copy.start()
        return copy

    key_copy, value_copy = fetch(key_in, key), fetch(value_in, value)
    cot_copy = fetch(cot, full_cot.at[tp])
    table_copies = [fetch(ahead_in, ahead), fetch(taps_in, taps), fetch(skip_in, skip)]
    state_copies = [fetch(behind_in, behind), fetch(query_in, query)]
    key_copy.wait()
    value_copy.wait()
    mixed[...] = (key[...].astype(F32) * value[...].astype(F32)).astype(BF16)
    pl.semaphore_wait(barrier, len(greeted))

    numbers = itertools.count()
    started = []

    def describe(source, target_ref, target, number, out_number):
        return pltpu.make_async_remote_copy(
            src_ref=source,
            dst_ref=target_ref,
            send_sem=send_sem.at[out_number],
            recv_sem=recv_sem.at[number],
            device_id=target,
            device_id_type=pl.DeviceIdType.MESH,
        )

    def send(source, target_ref, target, group=None, out=None):
        size = math.prod(source.shape) * source.dtype.itemsize
        if out is None:
            if not started or started[-1] >= SENT_ROWS * 2048 and planes_of(started[-1]):
                started.append(0)
            started[-1] += size
        number = next(numbers) if group is None else group[1]
        out_number = OUT_EXTRA + len(started) - 1 if out is None else out
        copy = describe(source, target_ref, target, number, out_number)
        copy.start()
        return copy

    def gather(landed):
        number = next(numbers)
        return describe(landed, landed, to_core, number, 0), number

    top, bottom = pl.ds(0, 128), pl.ds(128, 128)

    def pass_cot(owner, part, target):
        spot = full_cot.at[owner, part]
        return send(spot, spot, target)

    right_top = send(cot.at[top], full_cot.at[tp, top], to_right)
    left_bottom = send(cot.at[bottom], full_cot.at[tp, bottom], to_left)

    def weight_rows(low, odd, core):
        return pl.ds(pl.multiple_of(((low * 2 + odd) * 2 + core) * 128, 128), 128)

    odd = lax.rem(z, 2)
    given = weight_rows(1 - y[0], odd, core)
    imports = []
    for i in range(2):
        for r in range(4):
            rows = pl.ds(pl.multiple_of(given.start + r * 32, 32), 32)
            source = weight.at[rows, pl.ds(i * 1024, 1024)]
            imports.append(send(source, full_weight.at[dp * 2 + i, rows], to_far))
    right_bottom = send(cot.at[bottom], full_cot.at[tp, bottom], to_right)
    left_top = send(cot.at[top], full_cot.at[tp, top], to_left)
    own = [fetch(weight.at[:, pl.ds(i * 1024, 1024)], full_weight.at[dp * 2 + i]) for i in range(2)]

    wide = [pl.ds(h * 2 * TILE, 2 * TILE) for h in range(2)]
    mixed_sent = [send(mixed.at[bottom, cols], mixed_halo.at[:, cols], to_next) for cols in wide]

    def turn(owner, start, size):
        tokens, far_tokens = pl.ds(start, size), pl.ds(ROWS + start, size)
        for i in range(4):
            mine = pl.ds(pl.multiple_of((i * 2 + core) * 128, 128), 128)
            other = pl.ds(pl.multiple_of((i * 2 + 1 - core) * 128, 128), 128)
            turned[owner * 4 + i, :, tokens] = full_cot[owner, tokens, mine].T
            turned_away[owner * 4 + i, :, tokens] = full_cot[owner, tokens, other].T
        group = pl.ds(owner * 4, 4)
        return send(turned_away.at[group, :, tokens], turned.at[group, :, far_tokens], to_core)

    cot_copy.wait()
    turned_own = turn(tp, 0, ROWS)

    def columns(tile):
        return pl.ds(pl.multiple_of(tile * TILE, TILE), TILE)

    def spectrum(start, block):
        table = ahead[:, pl.ds(start, 2 * block.shape[0])]
        return matmul(table, jnp.concatenate([block, block], axis=0))

    def restore(places, real, imag):
        spec = jnp.concatenate([real, imag], axis=0)
        high = spec.astype(BF16)
        low = (spec - high.astype(F32)).astype(BF16)
        return matmul(behind[places], jnp.concatenate([high, high, low], axis=0))

    for copy in table_copies:
        copy.wait()

    @pl.loop(0, CHANNELS // TILE)
    def _(tile):
        cols = columns(tile)
        block = taps[cols]
        table = ahead[:, pl.ds(EARLY_HALO, 2 * TAPS)]
        spec = matmul_nt(table, jnp.concatenate([block, block], axis=1))
        tap_spec[pl.ds(0, HALF), cols] = spec[:HALF] + skip[:, cols]
        tap_spec[pl.ds(HALF, HALF), cols] = spec[HALF:]
        mixed_spec[:, cols] = spectrum(LATE_BLOCK, mixed[:, cols])

    def block_rows(kind, core):
        low = y[0] if kind in ("here", "above") else 1 - y[0]
        return weight_rows(low, odd if kind in ("here", "beside") else 1 - odd, core)

    kinds = ("here", "beside", "above", "corner")
    others = pl.ds((1 - dp) * 2, 2)
    from_core = {kind: gather(full_weight.at[others, block_rows(kind, 1 - core)]) for kind in kinds}
    from_side = gather(full_weight.at[others, block_rows("above", core)])
    from_corner = [
        gather(full_weight.at[(1 - dp) * 2 + i, block_rows("corner", core)]) for i in range(2)
    ]
    near_copies = []

    def weight_spot(kind, number):
        part = pl.ds(pl.multiple_of(block_rows(kind, core).start + number % 4 * 32, 32), 32)
        return full_weight.at[(1 - dp) * 2 + number // 4, part]

    def share_core(kind, i):
        spot = full_weight.at[(1 - dp) * 2 + i, block_rows(kind, core)]
        send(spot, spot, to_core, from_core[kind])

    def share_import(number):
        imports[number].wait_recv()
        spot = weight_spot("here", number)
        near_copies.append(send(spot, spot, to_near))
        send(spot, spot, to_side[number % 2], from_side)
        if number % 4 == 3:
            share_core("here", number // 4)

    def share_near(number):
        near_copies[number].wait_recv()
        spot = weight_spot("beside", number)
        send(spot, spot, to_side[number % 2], from_corner[number // 4])
        if number % 4 == 3:
            share_core("beside", number // 4)

    def convolve(start):
        @pl.loop(start, start + 2)
        def _(tile):
            cols = columns(tile)
            halo = jnp.where(seq > 0, mixed_halo[:, cols], jnp.zeros((TAPS, TILE), BF16))
            spec = mixed_spec[:, cols] + spectrum(EARLY_HALO, halo)
            mixed_spec[:, cols] = spec
            real, imag = spec[:HALF], spec[HALF:]
            tap_real, tap_imag = tap_spec[pl.ds(0, HALF), cols], tap_spec[pl.ds(HALF, HALF), cols]
            value_now = restore(
                pl.ds(0, ROWS),
                real * tap_real - imag * tap_imag,
                real * tap_imag + imag * tap_real,
            )
            state[:, cols] = value_now
            gated[pl.ds(0, ROWS), cols] = (query[:, cols].astype(F32) * value_now).astype(BF16)

    for copy in state_copies:
        copy.wait()
    gated_sent = []
    for h in range(2):
        mixed_sent[h].wait_recv()
        convolve(2 * h)
        half = gated.at[pl.ds(0, ROWS), wide[h]]
        gated_sent.append(send(half, gated.at[pl.ds(ROWS, ROWS), wide[h]], to_core))

    first = [
        [gather(landing[quarter * PER_QUARTER + stream]) for stream in range(STREAMS)]
        for quarter in range(4)
    ]

    def lanes_of(stream):
        return pl.ds(stream * LANES, LANES)

    def first_view(quarter, slot, stream):
        if quarter < 2:
            return partial.at[quarter, slot[0], slot[1], slot[2], :, lanes_of(stream)]
        return partial.at[quarter, slot[0], slot[1], :, :, lanes_of(stream)]

    def first_landing(quarter, chunk, i, stream):
        landed = landing[quarter * PER_QUARTER + stream]
        return landed.at[chunk] if quarter < 2 else landed.at[chunk, i]

    first_targets = [to_near, to_far, to_side[0], to_side[1]]

    def products(owner, start=0, stop=4):
        low, group = lax.div(owner, 2), pl.ds(lax.rem(owner, 2) * 4, 4)

        @pl.loop(start, stop)
        def _(quarter):
            rows = turned[pl.ds(owner * 4, 4)].reshape(512, 2 * ROWS)
            block = matmul(rows, gated[:, columns(quarter)]).astype(BF16)
            partial[quarter, low, group] = block.reshape(4, 2, 64, TILE)

    def halve(chunk, owner, stream, quarters=(0, 1, 2, 3)):
        for quarter in quarters:
            for i, slot in enumerate(first_slots(quarter, owner, y, z, False)):
                send(
                    first_view(quarter, slot, stream),
                    first_landing(quarter, chunk, i, stream),
                    first_targets[quarter],
                    first[quarter][stream],
                )

    share_import(0)
    share_import(1)
    turned_own.wait_recv()
    gated_sent[0].wait_recv()
    products(tp, 0, 2)
    halve(0, tp, 0, (0, 1))
    halve(0, tp, 1, (1,))
    share_import(2)
    gated_sent[1].wait_recv()
    products(tp, 2, 4)
    for stream in range(STREAMS):
        halve(0, tp, stream, (2, 3))
    right_top.wait_recv()
    forward_right = pass_cot(left, top, to_right)
    left_bottom.wait_recv()
    forward_left = pass_cot(right, bottom, to_left)
    share_import(3)
    share_near(0)
    turned_left = [turn(left, 0, 128)]
    turned_right = [turn(right, 128, 128)]
    share_import(4)
    share_import(5)
    share_import(6)
    right_bottom.wait_recv()
    turned_left.append(turn(left, 128, 128))
    left_top.wait_recv()
    turned_right.append(turn(right, 0, 128))
    share_import(7)
    share_near(1)
    share_near(2)
    for copy in own:
        copy.wait()
    late = jnp.where(lax.div(across, 2) == dp, across, dp * 4 + 1 - tp)
    early = dp * 4 + 1 - late

    @pl.loop(0, CHANNELS // TILE)
    def _(tile):
        cols = columns(tile)
        grad_gated[:, cols] = matmul_nt(full_cot[early], full_weight[early, cols])

    share_near(3)
    for copy in turned_left:
        copy.wait_recv()
    products(left)
    halve(1, left, 0)
    share_near(4)
    share_near(5)
    for copy in turned_right:
        copy.wait_recv()
    products(right)
    halve(2, right, 0)
    forward_right.wait_recv()
    forward_left.wait_recv()
    turned_across = turn(across, 0, ROWS)
    share_near(6)
    share_near(7)
    halve(0, tp, 1, (0,))
    halve(1, left, 1)
    @pl.loop(0, CHANNELS // TILE)
    def _(tile):
        cols = columns(tile)
        grad_gated[:, cols] += matmul_nt(full_cot[late], full_weight[late, cols])

    turned_across.wait_recv()
    products(across)
    halve(3, across, 0)
    halve(2, right, 1)
    halve(3, across, 1)

    from_side[0].wait_recv()
    share_core("above", 0)
    share_core("above", 1)
    from_corner[0][0].wait_recv()
    share_core("corner", 0)
    signal_sent = gather(signal_halo)
    near_sums = gather(near_land)

    def finish(tile, kind):
        from_core[kind][0].wait_recv()
        cols = columns(tile)
        total = grad_gated[:, cols]
        for i in range(2):
            owner = (1 - dp) * 2 + i
            total = total + matmul_nt(full_cot[owner], full_weight[owner, cols])
        made_query[:, cols] = (total * state[:, cols]).astype(BF16)
        signal[:, cols] = (total * query[:, cols].astype(F32)).astype(BF16)
        send(signal.at[top, cols], signal_halo.at[:, cols], to_prior, signal_sent)
        spec = spectrum(EARLY_BLOCK, signal[:, cols])
        signal_spec[:, cols] = spec
        real, imag = spec[:HALF], spec[HALF:]
        part_real, part_imag = mixed_spec[pl.ds(0, HALF), cols], mixed_spec[pl.ds(HALF, HALF), cols]
        lags = restore(
            pl.ds(2 * ROWS, TAPS),
            real * part_real + imag * part_imag,
            imag * part_real - real * part_imag,
        )
        for i in range(TILE // 128):
            block = lags[:, i * 128 : (i + 1) * 128].T
            owner = tile * 2 + i
            ahead_by = lax.rem(owner + 8 - member, 8)
            lag_sum[owner] = block.astype(BF16)

            @pl.when(ahead_by > 0)
            def _():
                send(
                    lag_sum.at[owner], near_land.at[ahead_by - 1], to_member(owner), near_sums, 0
                )


    rounds = {}

    def exchange(quarter, step, stream):
        axis, move = PLANS[quarter][step]
        there_y = move(y) if axis == "y" else y
        there_z = move(z) if axis == "z" else z
        landed = landing[quarter * PER_QUARTER + step * STREAMS + stream]
        group = gather(landed)
        for i, slot in enumerate(slots(PLANS[quarter], step, there_y, there_z)):
            view = slot_view(partial, quarter, slot, lanes_of(stream))
            send(view, landed.at[i], place(there_y, there_z, core), group)
        rounds[quarter, step, stream] = group[0], landed

    def combine(quarter, step, stream):
        lanes = lanes_of(stream)
        if step == 0:
            first[quarter][stream][0].wait_recv()
            pairs = [
                (first_view(quarter, slot, stream), first_landing(quarter, chunk, i, stream))
                for chunk, owner in enumerate((tp, left, right, across))
                for i, slot in enumerate(first_slots(quarter, owner, y, z, True))
            ]
        else:
            copy, landed = rounds[quarter, step, stream]
            copy.wait_recv()
            pairs = [
                (slot_view(partial, quarter, slot, lanes), landed.at[i])
                for i, slot in enumerate(slots(PLANS[quarter], step, y, z))
            ]
        for view, landed in pairs:
            total = view[...].astype(F32) + landed[...].astype(F32)
            if step < 4:
                view[...] = total.astype(BF16)
            else:
                place_out = pl.ds(quarter * TILE + stream * LANES, LANES)
                made_weight[:, place_out] = total * scale
        if step < 4:
            exchange(quarter, step + 1, stream)

    def combine_all(step, stream):
        for quarter in range(4):
            combine(quarter, step, stream)

    def restore_back(start):
        @pl.loop(start, start + 2)
        def _(tile):
            cols = columns(tile)
            halo = jnp.where(seq < 31, signal_halo[:, cols], jnp.zeros((TAPS, TILE), BF16))
            spec = signal_spec[:, cols] + spectrum(LATE_HALO, halo)
            real, imag = spec[:HALF], spec[HALF:]
            tap_real, tap_imag = tap_spec[pl.ds(0, HALF), cols], tap_spec[pl.ds(HALF, HALF), cols]
            back = restore(
                pl.ds(ROWS, ROWS),
                real * tap_real + imag * tap_imag,
                imag * tap_real - real * tap_imag,
            )
            made_key[:, cols] = (back * value[:, cols].astype(F32)).astype(BF16)
            made_value[:, cols] = (back * key[:, cols].astype(F32)).astype(BF16)

    finish(y[0] * 2 + odd, "here")
    finish((1 - y[0]) * 2 + odd, "beside")
    combine_all(0, 0)
    from_corner[1][0].wait_recv()
    share_core("corner", 1)
    finish(y[0] * 2 + 1 - odd, "above")
    finish((1 - y[0]) * 2 + 1 - odd, "corner")

    combine_all(0, 1)
    combine_all(1, 0)
    near_sums[0].wait_recv()
    total = lag_sum[member].astype(F32)
    for i in range(7):
        total = total + near_land[i].astype(F32)
    lag_mid[...] = total.reshape(8, 16, TAPS)
    far_sums = gather(far_land)
    for i in range(1, 8):
        send(lag_mid.at[heights[i]], far_land.at[i - 1], place(y, heights[i], core), far_sums, 1)

    signal_sent[0].wait_recv()

    restore_back(0)
    combine_all(1, 1)
    far_sums[0].wait_recv()
    total = lag_mid[z]
    for i in range(7):
        total = total + far_land[i]
    lag_out[member, z] = (total * scale).astype(BF16)
    mine = lag_out.at[member, z]
    copies = [send(mine, mine, place(y, heights[i], core), None, 2) for i in range(1, 8)]
    combine_all(2, 0)
    restore_back(2)
    combine_all(2, 1)
    for copy in copies:
        copy.wait_recv()
    mine = lag_out.at[member]
    copies = [send(mine, mine, to_member(members[i]), None, 3) for i in range(1, 8)]
    combine_all(3, 0)
    combine_all(3, 1)
    combine_all(4, 0)
    for copy in copies:
        copy.wait_recv()
    made_filter[...] = lag_out[...].astype(F32)
    diagonal = lax.broadcasted_iota(jnp.int32, (128, 128), 0) == lax.broadcasted_iota(
        jnp.int32, (128, 128), 1
    )
    for i in range(8):
        first_lag = made_filter[i].reshape(128, TAPS)[:, 0:1]
        spread = jnp.where(diagonal, jnp.broadcast_to(first_lag, (128, 128)), 0.0)
        made_skip[pl.ds(i, 1)] = jnp.sum(spread, axis=0, keepdims=True)
    combine_all(4, 1)
    sent = [near_land, far_land, near_land.at[:, pl.ds(0, 16)], near_land]
    for size in started:
        planes = planes_of(size)
        sent.append(full_weight.at[pl.ds(0, planes), pl.ds(0, size // 2048 // planes)])
    for out_number, block in enumerate(sent):
        describe(block, block, to_core, 0, out_number).wait_send()


def hand_on(*refs):
    count = (len(refs) - 1) // 2
    copies = [
        pltpu.make_async_copy(refs[i], refs[count + i], refs[-1].at[i]) for i in range(count)
    ]
    for copy in copies:
        copy.start()
    for copy in copies:
        copy.wait()


def per_device(query_gate, key_gate, value_input, filter_taps, skip_gain, out_weight, cotangent):
    ahead, behind = spectrum_tables()
    anywhere = pl.BlockSpec(memory_space=pl.ANY)
    block = ((ROWS, CHANNELS), BF16)
    scratch = [
        block,
        block,
        block,
        ((CHANNELS, TAPS), BF16),
        ((1, CHANNELS), F32),
        (ahead.shape, BF16),
        (behind.shape, BF16),
        ((4, ROWS, 1024), BF16),
        ((4, CHANNELS, 1024), BF16),
        ((16, 128, 2 * ROWS), BF16),
        ((16, 128, ROWS), BF16),
        ((2 * ROWS, CHANNELS), BF16),
        block,
        ((TAPS, CHANNELS), BF16),
        block,
        ((TAPS, CHANNELS), BF16),
        ((SIZE, CHANNELS), F32),
        ((SIZE, CHANNELS), F32),
        ((SIZE, CHANNELS), F32),
        ((ROWS, CHANNELS), F32),
        ((ROWS, CHANNELS), F32),
        ((4, 2, 8, 2, 64, TILE), BF16),
        ((8, 128, TAPS), BF16),
        ((8, 8, 16, TAPS), BF16),
        ((7, 128, TAPS), BF16),
        ((8, 16, TAPS), F32),
        ((7, 16, TAPS), F32),
    ]
    results = pl.pallas_call(
        kernel,
        out_shape=[
            pltpu.VMEM((ROWS, CHANNELS), BF16),
            pltpu.VMEM((ROWS, CHANNELS), BF16),
            pltpu.VMEM((ROWS, CHANNELS), BF16),
            pltpu.VMEM((8, 8, 16, TAPS), F32),
            pltpu.VMEM((8, 128), F32),
            pltpu.VMEM((64, CHANNELS), F32),
        ],
        in_specs=[anywhere] * 9,
        out_specs=[pl.BlockSpec(memory_space=pltpu.VMEM)] * 6,
        scratch_shapes=[pltpu.VMEM(shape, dtype) for shape, dtype in scratch]
        + [
            pltpu.SemaphoreType.DMA((OUT_EXTRA + OUT_SETS,)),
            pltpu.SemaphoreType.DMA((COPIES,)),
            pltpu.SemaphoreType.DMA((10,)),
        ]
        + [pltpu.VMEM(shape, BF16) for shape in landing_shapes()],
        compiler_params=pltpu.CompilerParams(
            collective_id=0, has_side_effects=True, vmem_limit_bytes=56 * 1024 * 1024
        ),
    )(
        query_gate[0], key_gate[0], value_input[0], filter_taps, skip_gain[None, :],
        out_weight, cotangent[0], jnp.asarray(ahead), jnp.asarray(behind),
    )
    results = [
        results[0][None],
        results[1][None],
        results[2][None],
        results[3].reshape(CHANNELS, TAPS),
        results[4].reshape(CHANNELS),
        results[5],
    ]
    return tuple(
        pl.pallas_call(
            hand_on,
            out_shape=[jax.ShapeDtypeStruct(x.shape, x.dtype) for x in results],
            in_specs=[pl.BlockSpec(memory_space=pltpu.VMEM)] * 6,
            out_specs=[anywhere] * 6,
            scratch_shapes=[pltpu.SemaphoreType.DMA((6,))],
        )(*[pltpu.with_memory_space_constraint(x, pltpu.VMEM) for x in results])
    )


def solution(mesh):
    return jax.shard_map(
        per_device,
        mesh=mesh,
        in_specs=(
            P("dp", "seq", "tp"),
            P("dp", "seq", "tp"),
            P("dp", "seq", "tp"),
            P("tp", None),
            P("tp"),
            P("tp", "dp"),
            P("dp", "seq", "tp"),
        ),
        out_specs=(
            P("dp", "seq", "tp"),
            P("dp", "seq", "tp"),
            P("dp", "seq", "tp"),
            P("tp", None),
            P("tp"),
            P(("seq", "dp"), "tp"),
        ),
        check_vma=False,
    )
```
